32 devices in a mesh: row: 4 (over y, core), col: 4 (over z), rep: 2 (over x).
Axes of the slice: x: 2, y: 2, z: 4, core: 2. Of those that a mesh axis runs over, the one named last changes fastest.
Arguments:
- precision: float32 [12288, 12288], P('row', 'col'), may hold values from -1 to 4, as said below
- samples: float32 [1024, 12288], P('rep', 'col'), may hold values from -6 to 6
- new_rows: float32 [512, 12288], P(None, 'row'), may hold values from -6 to 6
- ngram_order: int32 [12288], replicated, may hold values from 1 to 3
Outputs:
- updated: float32 [12288, 12288], P('row', ('col', 'rep'))
- residuals: float32 [512, 12288], P('row', ('col', 'rep'))
The draws below stay inside these ranges and needn't reach their ends.
Inputs may be any that keep to these rules, and one draw needn't show every extreme that they name: `precision`: symmetric; diagonal entries from 1 to 4, off-diagonal entries of magnitude at most 9 / sqrt(12288).
All inputs are finite; a program needn't handle non-finite values.
Results may differ from the reference program's by a relative error of at most 0.0003.
Values sent between devices are 32-bit elements; how exact they have to be, the bound alone decides.
A program may use at most 192 MiB of HBM per device.

```python
import math
import jax
import jax.numpy as jnp
from jax import lax

P_SIZE = 12288
NEW = 512
SAMPLES = 1024


def draw_precision(key, part):
    first_key, second_key = jax.random.split(key)
    spread = 3.0 / math.sqrt(P_SIZE)
    entries = jax.random.truncated_normal(first_key, -3.0, 3.0, (P_SIZE, P_SIZE), jnp.float32) * spread
    offdiag = (entries + entries.T) * 0.5
    diagonal = jnp.exp(jax.random.uniform(second_key, (P_SIZE,), jnp.float32, 0.0, math.log(4.0)))
    indices = jnp.arange(P_SIZE)
    return jnp.where(indices[:, None] == indices[None, :], diagonal[None, :], offdiag)


def set_ends(values, own_key, smallest, top_value):
    longest = values.shape.index(max(values.shape))
    spots = []
    for shift in (0, 1):
        where = [jax.random.randint(jax.random.fold_in(own_key, axis), (), 0, length) for axis, length in enumerate(values.shape)]
        where[longest] = (where[longest] + shift) % values.shape[longest]
        spots.append(tuple(where))
    return values.at[spots[0]].set(smallest).at[spots[1]].set(top_value)


def block_levels(own_key, shape, pieces, low, largest):
    factor_of = 1.0
    for position, shards_of in pieces:
        draws = jax.random.uniform(jax.random.fold_in(jax.random.fold_in(own_key, 6), position), (shards_of,), jnp.float32, low / len(pieces), largest / len(pieces))
        factor_of = factor_of * jnp.repeat(jnp.exp(draws), shape[position] // shards_of).reshape((-1,) + (1,) * (len(shape) - 1 - position))
    return factor_of


def gaussian(key, dims, scale, reach, cuts=(), dtype=jnp.bfloat16):
    values = scale * jax.random.normal(key, dims, jnp.float32)
    if cuts:
        values = values * block_levels(key, dims, cuts, -0.22, 0.18)
    return jnp.clip(values, -reach, reach).astype(dtype)


def setup_inputs(seed: int = 0) -> dict:
    arg_keys = jax.random.split(jax.random.key(seed), 5)
    return {
        "precision": draw_precision(jax.random.fold_in(arg_keys[4], 71), 0),
        "samples": gaussian(arg_keys[1], (SAMPLES, P_SIZE), 1.0, 6.0, ((0, 2), (1, 4)), jnp.float32),
        "new_rows": gaussian(arg_keys[2], (NEW, P_SIZE), 1.0, 6.0, ((1, 4),), jnp.float32),
        "ngram_order": set_ends(jax.random.randint(arg_keys[3], (P_SIZE,), 1, 4), jax.random.fold_in(arg_keys[3], 1), 1, 3).astype(jnp.int32),
    }


step_size = 0.25
penalty = 0.08


def contract(left, right, left_dim, right_dim):
    return lax.dot_general(left, right, (((left_dim,), (right_dim,)), ((), ())), preferred_element_type=jnp.float32, precision=lax.Precision.HIGHEST)


def reference(precision, samples, new_rows, ngram_order):
    sample_count = samples.shape[0]
    products = contract(precision, samples, 1, 1)
    diagonal = jnp.diagonal(precision)
    orders = ngram_order.astype(jnp.float32)
    block_size = math.gcd(P_SIZE, 1024)
    offsets = (jnp.arange(P_SIZE // block_size) * block_size).astype(jnp.int32)
    columns = jnp.arange(P_SIZE).astype(jnp.int32)

    def update_block(offset):
        prec_rows = lax.dynamic_slice_in_dim(precision, offset, block_size, 0)
        prod_rows = lax.dynamic_slice_in_dim(products, offset, block_size, 0)
        samp_cols = lax.dynamic_slice_in_dim(samples, offset, block_size, 1)
        symmetric = contract(prod_rows, samples, 1, 0) + contract(samp_cols, products, 0, 1)
        row_ids = offset + jnp.arange(block_size).astype(jnp.int32)
        on_diagonal = row_ids[:, None] == columns[None, :]
        inverse_diag = jnp.where(on_diagonal, 1.0 / jnp.where(on_diagonal, prec_rows, 1.0), 0.0)
        gradient = symmetric / (2.0 * sample_count) - inverse_diag
        stepped = prec_rows - step_size * gradient
        row_orders = lax.dynamic_slice_in_dim(orders, offset, block_size, 0)
        threshold = step_size * penalty * 0.5 * (row_orders[:, None] + orders[None, :])
        shrunk = jnp.sign(stepped) * jnp.maximum(jnp.abs(stepped) - threshold, 0.0)
        return jnp.where(on_diagonal, stepped, shrunk)

    updated = lax.map(update_block, offsets).reshape(P_SIZE, P_SIZE)
    residuals = contract(new_rows, updated, 1, 0) / diagonal[None, :]
    return updated, residuals
```

```python
import functools

import jax
import jax.numpy as jnp
from jax import lax
from jax.experimental import pallas as pl
from jax.experimental.pallas import tpu as pltpu
from jax.sharding import PartitionSpec as P

step_size = 0.25
penalty = 0.08
MESH = pl.DeviceIdType.MESH
F32 = jnp.float32
BF16 = jnp.bfloat16
step_rows = 128
chunk_rows = 64
depth = 256


def block_of(size):
    for block in (512, 384, 256, 128):
        if size % block == 0:
            return block
    return size


def split(values):
    high = values.astype(BF16)
    return high, (values - high.astype(F32)).astype(BF16)


def dot(left, right):
    return jnp.dot(left, right, preferred_element_type=F32)


def aligned(start, size, unit):
    return pl.ds(pl.multiple_of(start, unit), size)


def gather_kernel(
    R, C, S, TR, TC, H,
    prec, samp,
    acc_out, x_near, x_far, y_near, y_far, y_cols, x_cols_far, y_cols_far,
    acc, left, right, right_high, right_low, x_rows, partial, arrived, reduced,
    up_send, down_send, side_send, near_recv, far_recv,
    rs_send, rs_recv, ag_send, ag_recv, own_copy,
    xq_send, xq_recv, xf_send, xf_recv, yq_send, yq_recv, yf_send, yf_recv,
    om_sem, load_sem, out_sem,
):
    r, z, p = lax.axis_index("row"), lax.axis_index("col"), lax.axis_index("rep")
    ratio = TC // TR
    other = 1 - p
    source = r // ratio
    offset = (r % ratio) * TR
    is_source = z == source
    has_up = jnp.logical_and(z >= source, z < C - 1)
    has_down = jnp.logical_and(z <= source, z > 0)
    steps = S // step_rows
    chunks = S // chunk_rows
    per_step = step_rows // chunk_rows
    piece = step_rows // R
    quarter = S // R
    own_cols = aligned(p * H, H, 128)
    far_cols = aligned(other * H, H, 128)
    tile_cols = aligned(offset, TR, 128)

    def mate(d):
        return lax.rem(r + d, R)

    def remote(src, dst, send, recv, where):
        return pltpu.make_async_remote_copy(
            src_ref=src, dst_ref=dst, send_sem=send, recv_sem=recv, device_id=where, device_id_type=MESH
        )

    across = (r, z, other)

    barrier = pltpu.get_barrier_semaphore()
    pl.semaphore_signal(barrier, inc=1, device_id=across, device_id_type=MESH)
    for d in range(1, R):
        pl.semaphore_signal(barrier, inc=1, device_id=(mate(d), z, p), device_id_type=MESH)

    for hop in (1, C - 1):
        pl.semaphore_signal(barrier, inc=1, device_id=(r, lax.rem(z + hop, C), p), device_id_type=MESH)
    pl.semaphore_wait(barrier, R + 2)

    kinds = ((samp, x_near, x_far), (y_cols, y_near, y_far))

    def near_copies(kind, i, wide):
        wide_ref, near, far = kinds[kind]
        rows = aligned(i * chunk_rows, chunk_rows, chunk_rows)
        src = wide_ref.at[rows, tile_cols] if wide else near.at[rows]
        up = remote(src, near.at[rows], up_send.at[kind, i], near_recv.at[kind, i], (r, z + 1, p))
        down = remote(src, near.at[rows], down_send.at[kind, i], near_recv.at[kind, i], (r, z - 1, p))
        side = remote(src, far.at[rows], side_send.at[kind, i], far_recv.at[kind, i], across)
        return up, down, side

    def pass_on(kind, i, wide):
        up, down, side = near_copies(kind, i, wide)

        @pl.when(has_up)
        def _():
            up.start()

        @pl.when(has_down)
        def _():
            down.start()

        side.start()

    def start_source(kind, i):
        @pl.when(is_source)
        def _():
            pass_on(kind, i, True)

    def serve(kind, i):
        @pl.when(jnp.logical_not(is_source))
        def _():
            near_copies(kind, i, False)[0].wait_recv()
            pass_on(kind, i, False)

    def wait_far(kind, i):
        near_copies(kind, i, False)[2].wait_recv()

    def wait_sent(kind, i):
        up, down, side = near_copies(kind, i, False)

        @pl.when(has_up)
        def _():
            up.wait_send()

        @pl.when(has_down)
        def _():
            down.wait_send()

        side.wait_send()

    def xq_copy():
        rows = aligned(r * quarter, quarter, 8)
        return remote(samp.at[rows, far_cols], x_cols_far.at[rows], xq_send, xq_recv, across)

    def xf_copy(d, sender):
        rows = aligned(sender * quarter, quarter, 8)
        return remote(x_cols_far.at[rows], x_cols_far.at[rows], xf_send.at[d], xf_recv.at[d], (mate(d), z, p))

    def rs_copy(s, slot, d):
        rows = aligned(mate(d) * piece, piece, 8)
        return remote(
            partial.at[slot, rows], arrived.at[s, d - 1], rs_send.at[s, d], rs_recv.at[s, d], (mate(d), z, p)
        )

    def step_piece(s, sender):
        return aligned(s * step_rows + sender * piece, piece, 8)

    def ag_copy(s, d, sender):
        return remote(
            reduced.at[s], y_cols.at[step_piece(s, sender)], ag_send.at[s, d], ag_recv.at[s, d], (mate(d), z, p)
        )

    def own_piece(s):
        return pltpu.make_async_copy(reduced.at[s], y_cols.at[step_piece(s, r)], own_copy.at[s])

    def yq_copy(s):
        return remote(
            reduced.at[s, :, far_cols], y_cols_far.at[step_piece(s, r)], yq_send.at[s], yq_recv.at[s], across
        )

    def yf_copy(s, d, sender):
        rows = step_piece(s, sender)
        return remote(y_cols_far.at[rows], y_cols_far.at[rows], yf_send.at[s, d], yf_recv.at[s, d], (mate(d), z, p))

    for i in range(chunks):
        start_source(0, i)
    xq_copy().start()

    def om_copy(b, slot):
        rows = aligned(b * depth, depth, depth)
        return pltpu.make_async_copy(prec.at[rows], left.at[slot, :, pl.ds(0, TC)], om_sem.at[slot])

    blocks = TR // depth
    wide_block = block_of(TC)

    def finish_rs(s, slot):
        for d in range(1, R):
            rs_copy(s, slot, d).wait_recv()
        total = partial[slot, aligned(r * piece, piece, 8)]
        for d in range(1, R):
            total = total + arrived[s, d - 1]
        reduced[s] = total
        own_piece(s).start()
        yq_copy(s).start()
        for d in range(1, R):
            ag_copy(s, d, r).start()

    def wait_ag(s):
        own_piece(s).wait()
        for d in range(1, R):
            ag_copy(s, d, lax.rem(r + R - d, R)).wait_recv()

    def source_step(s):
        for j in range(per_step):
            start_source(1, s * per_step + j)

    def forward_yf(s):
        yq_copy(s).wait_recv()
        for d in range(1, R):
            yf_copy(s, d, r).start()

    @pl.loop(0, steps)
    def _(s):
        slot = lax.rem(s, 2)
        om_copy(0, 0).start()
        for j in range(per_step):
            serve(0, s * per_step + j)
        rows = aligned(s * step_rows, step_rows, step_rows)

        @pl.when(is_source)
        def _():
            pltpu.make_async_copy(samp.at[rows, tile_cols], x_rows, load_sem.at[0]).start()

        @pl.when(jnp.logical_not(is_source))
        def _():
            pltpu.make_async_copy(x_near.at[rows], x_rows, load_sem.at[0]).start()

        @pl.when(s >= 2)
        def _():
            for d in range(1, R):
                rs_copy(s - 2, slot, d).wait_send()

        pltpu.make_async_copy(x_near.at[rows], x_rows, load_sem.at[0]).wait()

        @pl.loop(0, blocks)
        def _(b):
            here = lax.rem(b, 2)
            om_copy(b, here).wait()

            @pl.when(b + 1 < blocks)
            def _():
                om_copy(b + 1, 1 - here).start()

            high, low = split(x_rows[:, aligned(b * depth, depth, depth)])
            both = jnp.concatenate([high, low], axis=0)
            for n in range(TC // wide_block):
                cols = pl.ds(n * wide_block, wide_block)
                w_high, w_low = split(left[here, :, cols])
                pair = dot(both, w_high)
                value = pair[:step_rows] + pair[step_rows:] + dot(high, w_low)

                @pl.when(b == 0)
                def _():
                    partial[slot, :, cols] = value

                @pl.when(b > 0)
                def _():
                    partial[slot, :, cols] += value

        for d in range(1, R):
            rs_copy(s, slot, d).start()

        @pl.when(s >= 1)
        def _():
            finish_rs(s - 1, 1 - slot)

        @pl.when(s == 1)
        def _():
            xq_copy().wait_recv()
            for d in range(1, R):
                xf_copy(d, r).start()

        @pl.when(s >= 2)
        def _():
            wait_ag(s - 2)
            source_step(s - 2)
            forward_yf(s - 2)

    last = steps - 1
    serve(1, 0)
    serve(1, 1)
    finish_rs(last, last % 2)
    wait_ag(last - 1)
    source_step(last - 1)
    forward_yf(last - 1)
    serve(1, 2)
    wait_ag(last)
    source_step(last)
    serve(1, 3)
    forward_yf(last)

    m_block, n_block = block_of(TR), block_of(H)
    out_blocks = TR // m_block
    halves = S // depth
    group = depth // chunk_rows

    def out_copy(i):
        rows = aligned(i * m_block, m_block, m_block)
        return pltpu.make_async_copy(acc.at[rows], acc_out.at[rows], out_sem)

    def load(src_left, src_right):
        pltpu.make_async_copy(src_left, left.at[0, :, pl.ds(0, TR)], load_sem.at[0]).start()
        pltpu.make_async_copy(src_right, right, load_sem.at[1]).start()

    def near_ref(kind, rows):
        def run(src_right):
            @pl.when(is_source)
            def _():
                load(kinds[kind][0].at[rows, tile_cols], src_right)

            @pl.when(jnp.logical_not(is_source))
            def _():
                load(kinds[kind][1].at[rows], src_right)

        return run

    def begin(u):
        if u == 2:
            for s in range(steps):
                for d in range(1, R):
                    yf_copy(s, d, lax.rem(r + R - d, R)).wait_recv()
        if u == 5:
            for d in range(1, R):
                xf_copy(d, lax.rem(r + R - d, R)).wait_recv()
        served = {1: (4,), 3: (5,), 5: (6, 7)}.get(u, ())
        for i in served:
            serve(1, i)
        if u in (2, 3):
            for i in range(group):
                wait_far(0, (u - 2) * group + i)
        if u in (5, 7):
            for i in range(group):
                wait_far(1, (u - 5) // 2 * group + i)
        k = u % 2 if u < 4 else (u - 4) // 2
        rows = pl.ds(k * depth, depth)
        if u < 2:
            near_ref(0, rows)(y_cols.at[rows, own_cols])
        elif u < 4:
            load(x_far.at[rows], y_cols_far.at[rows])
        elif u % 2 == 0:
            near_ref(1, rows)(samp.at[rows, own_cols])
        else:
            load(y_far.at[rows], x_cols_far.at[rows])

    assert halves == 2 and chunks == 8 and per_step == 2

    @pl.loop(0, 8)
    def _(u):
        for case in range(8):
            @pl.when(u == case)
            def _(case=case):
                begin(case)

        pltpu.make_async_copy(x_far.at[pl.ds(0, depth)], left.at[0, :, pl.ds(0, TR)], load_sem.at[0]).wait()
        pltpu.make_async_copy(y_cols_far.at[pl.ds(0, depth)], right, load_sem.at[1]).wait()
        high, low = split(right[...])
        right_high[...] = high
        right_low[...] = low

        @pl.loop(0, out_blocks)
        def _(i):
            rows = aligned(i * m_block, m_block, m_block)
            l_high, l_low = split(left[0, :, rows].T)
            for n in range(H // n_block):
                cols = pl.ds(n * n_block, n_block)
                value = dot(l_high, right_high[:, cols]) + dot(l_low, right_high[:, cols])
                value = value + dot(l_high, right_low[:, cols])

                @pl.when(u == 0)
                def _():
                    acc[rows, cols] = value

                @pl.when(u > 0)
                def _():
                    acc[rows, cols] += value

            @pl.when(u == 7)
            def _():
                out_copy(i).start()

    @pl.loop(0, chunks)
    def _(i):
        wait_sent(0, i)
        wait_sent(1, i)

    xq_copy().wait_send()
    for d in range(1, R):
        xf_copy(d, r).wait_send()
    for s in range(steps):
        yq_copy(s).wait_send()
        for d in range(1, R):
            if s >= steps - 2:
                rs_copy(s, s % 2, d).wait_send()
            ag_copy(s, d, r).wait_send()
            yf_copy(s, d, r).wait_send()

    @pl.loop(0, out_blocks)
    def _(i):
        out_copy(i).wait()


def gathered(precision, samples, R, C):
    TR, TC = precision.shape
    S = samples.shape[0]
    H = TC // 2
    assert C > 2
    steps, chunks = S // step_rows, S // chunk_rows
    piece = step_rows // R
    wide = max(TR, TC)
    dma = pltpu.SemaphoreType.DMA
    shapes = [(TR, H), (S, TR), (S, TR), (S, TR), (S, TR), (S, TC), (S, H), (S, H)]
    return pl.pallas_call(
        functools.partial(gather_kernel, R, C, S, TR, TC, H),
        out_shape=[jax.ShapeDtypeStruct(shape, F32) for shape in shapes],
        in_specs=[pl.BlockSpec(memory_space=pl.ANY)] * 2,
        out_specs=[pl.BlockSpec(memory_space=pl.ANY)] * len(shapes),
        scratch_shapes=[
            pltpu.VMEM((TR, H), F32),
            pltpu.VMEM((2, depth, wide), F32),
            pltpu.VMEM((depth, H), F32),
            pltpu.VMEM((depth, H), BF16),
            pltpu.VMEM((depth, H), BF16),
            pltpu.VMEM((step_rows, TR), F32),
            pltpu.VMEM((2, step_rows, TC), F32),
            pltpu.VMEM((steps, R - 1, piece, TC), F32),
            pltpu.VMEM((steps, piece, TC), F32),
            dma((2, chunks)), dma((2, chunks)), dma((2, chunks)), dma((2, chunks)), dma((2, chunks)),
            dma((steps, R)), dma((steps, R)), dma((steps, R)), dma((steps, R)), dma((steps,)),
            dma, dma, dma((R,)), dma((R,)), dma((steps,)), dma((steps,)), dma((steps, R)), dma((steps, R)),
            dma((2,)), dma((2,)), dma,
        ],
        compiler_params=pltpu.CompilerParams(
            collective_id=0, has_side_effects=True, vmem_limit_bytes=60 * 2**20
        ),
        name="gather_symmetric",
    )(precision, samples)[0]


def update_kernel(samples_total, block, ids, sym, prec, rows_o, cols_o, new_t, out, res):
    i = pl.program_id(0)
    M, H = sym.shape
    row_id = ids[0] + i * block + lax.broadcasted_iota(jnp.int32, (M, H), 0)
    col_id = ids[1] + lax.broadcasted_iota(jnp.int32, (M, H), 1)
    on_diagonal = row_id == col_id
    held = prec[...]
    inverse = jnp.where(on_diagonal, 1.0 / jnp.where(on_diagonal, held, 1.0), 0.0)
    gradient = sym[...] / (2.0 * samples_total) - inverse
    stepped = held - step_size * gradient
    threshold = step_size * penalty * 0.5 * (rows_o[...] + cols_o[...])
    size = jnp.maximum(jnp.abs(stepped) - threshold, 0.0)
    shrunk = jnp.where(stepped < 0.0, -size, size)
    updated = jnp.where(on_diagonal, stepped, shrunk)
    out[...] = updated
    u_high, u_low = split(updated)
    n_high, n_low = split(new_t[...])
    count = n_high.shape[0]
    pair = dot(jnp.concatenate([n_high, n_low], axis=0), u_high)
    value = pair[:count] + pair[count:] + dot(n_high, u_low)
    diag = jnp.sum(jnp.where(on_diagonal, held, 0.0), axis=0, keepdims=True)
    diag = jnp.broadcast_to(diag, (8, H))

    @pl.when(i == 0)
    def _():
        res[pl.ds(0, count), :] = value
        res[pl.ds(count, 8), :] = diag

    @pl.when(i > 0)
    def _():
        res[pl.ds(0, count), :] += value
        res[pl.ds(count, 8), :] += diag


def updated_and_partial(symmetric, precision, new_rows, orders_rows, orders_cols, ids, half_index, samples_total):
    TR, H = symmetric.shape
    count = new_rows.shape[0]
    block = 256
    return pl.pallas_call(
        functools.partial(update_kernel, samples_total, block),
        out_shape=[jax.ShapeDtypeStruct((TR, H), F32), jax.ShapeDtypeStruct((count + 8, H), F32)],
        grid_spec=pltpu.PrefetchScalarGridSpec(
            num_scalar_prefetch=1,
            grid=(TR // block,),
            in_specs=[
                pl.BlockSpec((block, H), lambda i, ids: (i, 0)),
                pl.BlockSpec((block, H), lambda i, ids: (i, ids[2])),
                pl.BlockSpec((block, 1), lambda i, ids: (i, 0)),
                pl.BlockSpec((1, H), lambda i, ids: (0, 0)),
                pl.BlockSpec((count, block), lambda i, ids: (0, i)),
            ],
            out_specs=[
                pl.BlockSpec((block, H), lambda i, ids: (i, 0)),
                pl.BlockSpec((count + 8, H), lambda i, ids: (0, 0)),
            ],
        ),
        compiler_params=pltpu.CompilerParams(vmem_limit_bytes=56 * 2**20),
        name="update_rows",
    )(ids, symmetric, precision, orders_rows, orders_cols, new_rows)


def residual_kernel(R, part, out, held, got, diags, send, recv, diag_send, diag_recv):
    r, z, p = lax.axis_index("row"), lax.axis_index("col"), lax.axis_index("rep")
    rows = out.shape[0]
    rounds = R.bit_length() - 1

    def flip(bit):
        low = lax.rem(r // bit, 2)
        return r + bit - 2 * bit * low

    barrier = pltpu.get_barrier_semaphore()
    for d in range(1, R):
        where = (lax.rem(r + d, R), z, p)
        pl.semaphore_signal(barrier, inc=1, device_id=where, device_id_type=MESH)
    pl.semaphore_wait(barrier, R - 1)

    def diag_copy(d):
        where = (lax.rem(r + d, R), z, p)
        return pltpu.make_async_remote_copy(
            src_ref=part.at[pl.ds(rows * R, 8)], dst_ref=diags.at[d - 1], send_sem=diag_send.at[d],
            recv_sem=diag_recv.at[d], device_id=where, device_id_type=MESH)

    def exchange(stage, j):
        bit = 1 << stage
        peer = flip(bit)
        block = lax.rem(peer, 2 * bit) + 2 * bit * j
        src = part if stage == 0 else held
        return pltpu.make_async_remote_copy(
            src_ref=src.at[aligned(block * rows, rows, 8)], dst_ref=got.at[stage, j],
            send_sem=send.at[stage, j], recv_sem=recv.at[stage, j],
            device_id=(peer, z, p), device_id_type=MESH)

    count = [R >> (stage + 1) for stage in range(rounds)]
    for stage in range(rounds):
        bit = 1 << stage
        if stage == 0:
            for j in range(count[0]):
                exchange(0, j).start()
            for d in range(1, R):
                diag_copy(d).start()

        def receive(j, stage=stage, bit=bit):
            mine = lax.rem(r, 2 * bit) + 2 * bit * j
            block = aligned(mine * rows, rows, 8)
            exchange(stage, j).wait_recv()
            src = part if stage == 0 else held
            held[block] = src[block] + got[stage, j]

        for j in range(count[stage]):
            receive(j)
        if stage + 1 < rounds:
            for j in range(count[stage + 1]):
                exchange(stage + 1, j).start()
    diag = part[pl.ds(rows * R, 1)]
    for d in range(1, R):
        diag_copy(d).wait_recv()
        diag = diag + diags[d - 1, pl.ds(0, 1)]
    out[...] = held[aligned(r * rows, rows, 8)] / diag
    for stage in range(rounds):
        for j in range(count[stage]):
            exchange(stage, j).wait_send()
    for d in range(1, R):
        diag_copy(d).wait_send()


def residual_sum(part, R):
    total, H = part.shape
    rows = (total - 8) // R
    assert R & (R - 1) == 0
    rounds = R.bit_length() - 1
    dma = pltpu.SemaphoreType.DMA
    return pl.pallas_call(
        functools.partial(residual_kernel, R),
        out_shape=jax.ShapeDtypeStruct((rows, H), F32),
        in_specs=[pl.BlockSpec(memory_space=pltpu.VMEM)],
        out_specs=pl.BlockSpec(memory_space=pltpu.VMEM),
        scratch_shapes=[
            pltpu.VMEM((R * rows, H), F32),
            pltpu.VMEM((rounds, R // 2, rows, H), F32),
            pltpu.VMEM((R - 1, 8, H), F32),
            dma((rounds, R // 2)), dma((rounds, R // 2)), dma((R,)), dma((R,)),
        ],
        compiler_params=pltpu.CompilerParams(
            collective_id=1, has_side_effects=True, vmem_limit_bytes=40 * 2**20
        ),
        name="residual_sum",
    )(part)


def per_device(precision, samples, new_rows, ngram_order):
    R, C, reps = lax.axis_size("row"), lax.axis_size("col"), lax.axis_size("rep")
    r, c, p = lax.axis_index("row"), lax.axis_index("col"), lax.axis_index("rep")
    TR, TC = precision.shape
    H = TC // reps
    assert reps == 2 and TC % TR == 0 and R * TR == C * TC
    symmetric = gathered(precision, samples, R, C)
    orders = ngram_order.astype(F32)
    row_start, col_start = r * TR, c * TC + p * H
    order_rows = lax.dynamic_slice_in_dim(orders, row_start, TR, 0)[:, None]
    order_cols = lax.dynamic_slice_in_dim(orders, col_start, H, 0)[None, :]
    ids = jnp.stack([row_start, col_start, p]).astype(jnp.int32)
    updated, part = updated_and_partial(
        symmetric, precision, new_rows, order_rows, order_cols, ids, p, samples.shape[0] * reps
    )
    return updated, residual_sum(part, R)


def solution(mesh):
    placed = (P("row", "col"), P("rep", "col"), P(None, "row"), P())
    return jax.shard_map(
        per_device,
        mesh=mesh,
        in_specs=placed,
        out_specs=(P("row", ("col", "rep")), P("row", ("col", "rep"))),
        check_vma=False,
    )
```

```python
import functools

import jax
import jax.numpy as jnp
from jax import lax
from jax.experimental import pallas as pl
from jax.experimental.pallas import tpu as pltpu
from jax.sharding import PartitionSpec as P

step_size = 0.25
penalty = 0.08
MESH = pl.DeviceIdType.MESH
F32 = jnp.float32
BF16 = jnp.bfloat16
step_rows = 256
chunk_rows = 64
depth = 256
alternate = ((0, 5), (0, 7))


def block_of(size, most=512):
    for block in (1024, 768, 512, 384, 256, 128):
        if block <= most and size % block == 0:
            return block
    return size


def split(values):
    high = values.astype(BF16)
    return high, (values - high.astype(F32)).astype(BF16)


def dot(left, right):
    return jnp.dot(left, right, preferred_element_type=F32)


def aligned(start, size, unit):
    return pl.ds(pl.multiple_of(start, unit), size)


def gather_kernel(
    R, C, S, TR, TC, H,
    prec, samp,
    acc_out, x_near, x_far, y_near, y_far, y_cols, x_cols_far, y_cols_far, kept_rows,
    acc, left, right, right_high, right_low, x_rows, partial, paired, mid, arrived, reduced,
    up_send, down_send, side_send, near_recv, far_recv, alt_up, alt_down, alt_over, alt_recv,
    pair_send, pair_recv, rs_send, rs_recv, own_copy,
    share_send, share_recv, hand_send, hand_recv,
    xq_send, xq_recv, yq_send, yq_recv,
    om_sem, load_sem, out_sem,
):
    r, z, p = lax.axis_index("row"), lax.axis_index("col"), lax.axis_index("rep")
    ratio = TC // TR
    other = 1 - p
    source = r // ratio
    offset = (r % ratio) * TR
    is_source = z == source
    has_up = jnp.logical_and(z >= source, z < C - 1)
    has_down = jnp.logical_and(z <= source, z > 0)
    alt = lax.rem(r + R // 2, R)
    alt_source = alt // ratio
    is_alt_source = z == alt_source
    alt_has_up = jnp.logical_and(z >= alt_source, z < C - 1)
    alt_has_down = jnp.logical_and(z <= alt_source, z > 0)
    alt_cols = aligned((alt % ratio) * TR, TR, 128)
    steps = S // step_rows
    chunks = S // chunk_rows
    per_step = step_rows // chunk_rows
    piece = step_rows // R
    quarter = S // R
    own_cols = aligned(p * H, H, 128)
    far_cols = aligned(other * H, H, 128)
    tile_cols = aligned(offset, TR, 128)

    pairs = R // 2
    twin = r + 1 - 2 * lax.rem(r, 2)
    parity = lax.rem(r, 2)
    group_index = r // 2

    def mate(d):
        return lax.rem(r + d, R)

    def peer(e):
        return lax.rem(r + 2 * e, R)

    def sender_of(e):
        return lax.rem(r + R - 2 * e, R)

    def remote(src, dst, send, recv, where):
        return pltpu.make_async_remote_copy(
            src_ref=src, dst_ref=dst, send_sem=send, recv_sem=recv, device_id=where, device_id_type=MESH
        )

    across = (r, z, other)

    barrier = pltpu.get_barrier_semaphore()
    pl.semaphore_signal(barrier, inc=1, device_id=across, device_id_type=MESH)
    for d in range(1, R):
        pl.semaphore_signal(barrier, inc=1, device_id=(mate(d), z, p), device_id_type=MESH)

    for hop in (1, C - 1):
        pl.semaphore_signal(barrier, inc=1, device_id=(r, lax.rem(z + hop, C), p), device_id_type=MESH)
    pl.semaphore_wait(barrier, R + 2)

    kinds = ((samp, x_near, x_far), (y_cols, y_near, y_far))

    def near_copies(kind, i, wide):
        wide_ref, near, far = kinds[kind]
        rows = aligned(i * chunk_rows, chunk_rows, chunk_rows)
        src = wide_ref.at[rows, tile_cols] if wide else near.at[rows]
        up = remote(src, near.at[rows], up_send.at[kind, i], near_recv.at[kind, i], (r, z + 1, p))
        down = remote(src, near.at[rows], down_send.at[kind, i], near_recv.at[kind, i], (r, z - 1, p))
        side = remote(src, far.at[rows], side_send.at[kind, i], far_recv.at[kind, i], across)
        return up, down, side

    def pass_on(kind, i, wide):
        up, down, side = near_copies(kind, i, wide)

        @pl.when(has_up)
        def _():
            up.start()

        @pl.when(has_down)
        def _():
            down.start()

        side.start()

    def alt_copies(kind, i, wide):
        wide_ref, near, _ = kinds[kind]
        j = alternate.index((kind, i))
        rows = aligned(i * chunk_rows, chunk_rows, chunk_rows)
        kept = kept_rows.at[pl.ds(j * chunk_rows, chunk_rows)]
        src = wide_ref.at[rows, alt_cols] if wide else kept
        up = remote(src, kept, alt_up.at[j], alt_recv.at[j], (r, z + 1, p))
        down = remote(src, kept, alt_down.at[j], alt_recv.at[j], (r, z - 1, p))
        over = remote(kept, near.at[rows], alt_over.at[j], near_recv.at[kind, i], (alt, z, p))
        return up, down, over

    def pass_alt(kind, i, wide):
        up, down, _ = alt_copies(kind, i, wide)

        @pl.when(alt_has_up)
        def _():
            up.start()

        @pl.when(alt_has_down)
        def _():
            down.start()

    def start_source(kind, i):
        @pl.when(is_source)
        def _():
            if (kind, i) in alternate:
                near_copies(kind, i, True)[2].start()
            else:
                pass_on(kind, i, True)

        if (kind, i) in alternate:
            @pl.when(is_alt_source)
            def _():
                pass_alt(kind, i, True)

    def serve(kind, i):
        if (kind, i) in alternate:
            @pl.when(jnp.logical_not(is_alt_source))
            def _():
                alt_copies(kind, i, False)[0].wait_recv()
                pass_alt(kind, i, False)
                alt_copies(kind, i, False)[2].start()

        @pl.when(jnp.logical_not(is_source))
        def _():
            near_copies(kind, i, False)[0].wait_recv()
            if (kind, i) in alternate:
                near_copies(kind, i, False)[2].start()
            else:
                pass_on(kind, i, False)

    def wait_far(kind, i):
        near_copies(kind, i, False)[2].wait_recv()

    def wait_sent(kind, i):
        up, down, side = near_copies(kind, i, False)
        side.wait_send()
        if (kind, i) in alternate:
            up, down, over = alt_copies(kind, i, False)

            @pl.when(jnp.logical_not(is_alt_source))
            def _():
                over.wait_send()

        rises, falls = (alt_has_up, alt_has_down) if (kind, i) in alternate else (has_up, has_down)

        @pl.when(rises)
        def _():
            up.wait_send()

        @pl.when(falls)
        def _():
            down.wait_send()

    def xq_copy():
        rows = aligned(r * quarter, quarter, 8)
        return remote(samp.at[rows, far_cols], x_cols_far.at[rows], xq_send, xq_recv, across)

    def step_piece(s, owner):
        return aligned(s * step_rows + owner * piece, piece, 8)

    def pair_copy(s, slot, j):
        rows = aligned((2 * j + 1 - parity) * piece, piece, 8)
        return remote(
            partial.at[slot, rows], paired.at[s, j], pair_send.at[s, j], pair_recv.at[s, j], (twin, z, p)
        )

    def rs_copy(s, e):
        return remote(
            mid.at[s, peer(e) // 2], arrived.at[s, e - 1], rs_send.at[s, e], rs_recv.at[s, e], (peer(e), z, p)
        )

    def own_piece(s):
        return pltpu.make_async_copy(reduced.at[s], y_cols.at[step_piece(s, r)], own_copy.at[s])

    def yq_copy(s):
        return remote(
            reduced.at[s, :, far_cols], y_cols_far.at[step_piece(s, r)], yq_send.at[s], yq_recv.at[s], across
        )

    def shared(which, owner):
        if which == 2 * steps:
            return x_cols_far.at[aligned(owner * quarter, quarter, 8)]
        if which < steps:
            return y_cols.at[step_piece(which, owner)]
        return y_cols_far.at[step_piece(which - steps, owner)]

    def share_copy(which, e, owner, src=None):
        piece_ref = shared(which, owner)
        return remote(
            piece_ref if src is None else src, piece_ref,
            share_send.at[which, e], share_recv.at[which, e], (peer(e), z, p),
        )

    def hand_copy(which, owner, src=None):
        piece_ref = shared(which, owner)
        g = owner // 2
        return remote(
            piece_ref if src is None else src, piece_ref,
            hand_send.at[which, g], hand_recv.at[which, g], (twin, z, p),
        )

    def share(which, src=None):
        for e in range(1, pairs):
            share_copy(which, e, r, src).start()
        hand_copy(which, r, src).start()

    def hand_on(which):
        for e in range(1, pairs):
            owner = sender_of(e)
            share_copy(which, e, owner).wait_recv()
            hand_copy(which, owner).start()

    def wait_handed(which):
        for g in range(pairs):
            hand_copy(which, 2 * g + 1 - parity).wait_recv()

    def wait_shared(which):
        for e in range(1, pairs):
            share_copy(which, e, r).wait_send()
        for g in range(pairs):
            hand_copy(which, 2 * g + parity).wait_send()

    for i in range(chunks):
        start_source(0, i)
    xq_copy().start()

    def om_copy(b, slot):
        rows = aligned(b * depth, depth, depth)
        return pltpu.make_async_copy(prec.at[rows], left.at[slot, :, pl.ds(0, TC)], om_sem.at[slot])

    blocks = TR // depth
    wide_block = block_of(TC, 1024)

    def combine(s, slot):
        for j in range(pairs):
            pair_copy(s, slot, j).wait_recv()
            rows = aligned((2 * j + parity) * piece, piece, 8)
            mid[s, j] = partial[slot, rows] + paired[s, j]
        for e in range(1, pairs):
            rs_copy(s, e).start()

    def finish(s):
        total = mid[s, group_index]
        for e in range(1, pairs):
            rs_copy(s, e).wait_recv()
            total = total + arrived[s, e - 1]
        reduced[s] = total
        own_piece(s).start()
        share(s, reduced.at[s])
        yq_copy(s).start()

    def source_step(s):
        own_piece(s).wait()
        wait_handed(s)
        for j in range(per_step):
            start_source(1, s * per_step + j)

    def spread_far(s):
        yq_copy(s).wait_recv()
        share(steps + s)

    def load_x(s):
        rows = aligned(s * step_rows, step_rows, step_rows)

        @pl.when(is_source)
        def _():
            pltpu.make_async_copy(samp.at[rows, tile_cols], x_rows, load_sem.at[0]).start()

        @pl.when(jnp.logical_not(is_source))
        def _():
            pltpu.make_async_copy(x_near.at[rows], x_rows, load_sem.at[0]).start()

        pltpu.make_async_copy(x_near.at[rows], x_rows, load_sem.at[0]).wait()

    def products_step(slot):
        @pl.loop(0, blocks)
        def _(b):
            here = lax.rem(b, 2)
            om_copy(b, here).wait()

            @pl.when(b + 1 < blocks)
            def _():
                om_copy(b + 1, 1 - here).start()

            high, low = split(x_rows[:, aligned(b * depth, depth, depth)])
            both = jnp.concatenate([high, low], axis=0)
            for n in range(TC // wide_block):
                cols = pl.ds(n * wide_block, wide_block)
                w_high, w_low = split(left[here, :, cols])
                pair = dot(both, w_high)
                value = pair[:step_rows] + pair[step_rows:] + dot(high, w_low)

                @pl.when(b == 0)
                def _():
                    partial[slot, :, cols] = value

                @pl.when(b > 0)
                def _():
                    partial[slot, :, cols] += value

    def products(s):
        load_x(s)
        if s >= 2:
            for j in range(pairs):
                pair_copy(s - 2, s % 2, j).wait_send()
        products_step(s % 2)
        for j in range(pairs):
            pair_copy(s, s % 2, j).start()
        if s + 1 < steps:
            om_copy(0, 0).start()

    def serve_x(i):
        serve(0, i)

    def serve_y(i):
        serve(1, i)

    def mix(s):
        combine(s, s % 2)

    def spread_x(_):
        xq_copy().wait_recv()
        share(2 * steps)

    def hand_far(s):
        hand_on(steps + s)

    assert steps == 2 and chunks == 8
    om_copy(0, 0).start()
    order = (
        (serve_x, 0), (serve_x, 1), (serve_x, 2), (serve_x, 7), (serve_x, 3), (products, 0), (serve_x, 5),
        (mix, 0), (serve_x, 6), (finish, 0), (serve_x, 4), (hand_on, 0), (source_step, 0), (products, 1),
        (mix, 1), (serve_y, 1), (serve_y, 0), (finish, 1),
    )
    for action, index in order:
        action(index)
    terms = (0, 1, 2, 4, 5, 3, 6, 7)
    between = {
        1: (
            (spread_far, 0), (spread_x, 0), (hand_on, 1), (serve_y, 2), (serve_y, 3), (source_step, 1),
            (spread_far, 1),
        ),
        2: (
            (hand_far, 0), (hand_on, 2 * steps), (hand_far, 1), (serve_y, 4),
        ),
        3: (
            (serve_y, 5),
        ),
        5: (
            (serve_y, 6),
        ),
        6: (
            (serve_y, 7),
        ),
    }

    m_block, n_block = block_of(TR), block_of(H)
    out_blocks = TR // m_block
    halves = S // depth
    group = depth // chunk_rows

    def out_copy(i):
        rows = aligned(i * m_block, m_block, m_block)
        return pltpu.make_async_copy(acc.at[rows], acc_out.at[rows], out_sem)

    def load(src_left, src_right):
        pltpu.make_async_copy(src_left, left.at[0, :, pl.ds(0, TR)], load_sem.at[0]).start()
        pltpu.make_async_copy(src_right, right, load_sem.at[1]).start()

    def near_ref(kind, rows):
        def run(src_right):
            @pl.when(is_source)
            def _():
                load(kinds[kind][0].at[rows, tile_cols], src_right)

            @pl.when(jnp.logical_not(is_source))
            def _():
                load(kinds[kind][1].at[rows], src_right)

        return run

    def begin(place):
        u = terms[place]
        for action, index in between.get(place, ()):
            action(index)
        if u in (2, 3):
            for s in range(steps // 2):
                wait_handed(steps + (u - 2) * (steps // 2) + s)
        if u in (5, 7) and not {5, 7} & set(terms[:place]):
            wait_handed(2 * steps)
        if u in (2, 3):
            for i in range(group):
                wait_far(0, (u - 2) * group + i)
        if u in (5, 7):
            for i in range(group):
                wait_far(1, (u - 5) // 2 * group + i)
        k = u % 2 if u < 4 else (u - 4) // 2
        rows = pl.ds(k * depth, depth)
        if u < 2:
            near_ref(0, rows)(y_cols.at[rows, own_cols])
        elif u < 4:
            load(x_far.at[rows], y_cols_far.at[rows])
        elif u % 2 == 0:
            near_ref(1, rows)(samp.at[rows, own_cols])
        else:
            load(y_far.at[rows], x_cols_far.at[rows])

    assert halves == 2

    @pl.loop(0, 8)
    def _(u):
        for case in range(8):
            @pl.when(u == case)
            def _(case=case):
                begin(case)

        pltpu.make_async_copy(x_far.at[pl.ds(0, depth)], left.at[0, :, pl.ds(0, TR)], load_sem.at[0]).wait()
        pltpu.make_async_copy(y_cols_far.at[pl.ds(0, depth)], right, load_sem.at[1]).wait()
        high, low = split(right[...])
        right_high[...] = high
        right_low[...] = low

        @pl.loop(0, out_blocks)
        def _(i):
            rows = aligned(i * m_block, m_block, m_block)
            l_high, l_low = split(left[0, :, rows].T)
            for n in range(H // n_block):
                cols = pl.ds(n * n_block, n_block)
                value = dot(l_high, right_high[:, cols]) + dot(l_low, right_high[:, cols])
                value = value + dot(l_high, right_low[:, cols])

                @pl.when(u == 0)
                def _():
                    acc[rows, cols] = value

                @pl.when(u > 0)
                def _():
                    acc[rows, cols] += value

            @pl.when(u == 7)
            def _():
                out_copy(i).start()

    for i in range(chunks):
        wait_sent(0, i)
        wait_sent(1, i)

    xq_copy().wait_send()
    for which in range(2 * steps + 1):
        wait_shared(which)
    for s in range(steps):
        yq_copy(s).wait_send()
        for e in range(1, pairs):
            rs_copy(s, e).wait_send()
        if s >= steps - 2:
            for j in range(pairs):
                pair_copy(s, s % 2, j).wait_send()

    @pl.loop(0, out_blocks)
    def _(i):
        out_copy(i).wait()


def gathered(precision, samples, R, C):
    TR, TC = precision.shape
    S = samples.shape[0]
    H = TC // 2
    assert C > 2
    steps, chunks = S // step_rows, S // chunk_rows
    piece = step_rows // R
    pairs, shares = R // 2, 2 * steps + 1
    assert R % 2 == 0
    wide = max(TR, TC)
    dma = pltpu.SemaphoreType.DMA
    shapes = [(TR, H), (S, TR), (S, TR), (S, TR), (S, TR), (S, TC), (S, H), (S, H)]
    shapes.append((len(alternate) * chunk_rows, TR))
    return pl.pallas_call(
        functools.partial(gather_kernel, R, C, S, TR, TC, H),
        out_shape=[jax.ShapeDtypeStruct(shape, F32) for shape in shapes],
        in_specs=[pl.BlockSpec(memory_space=pl.ANY)] * 2,
        out_specs=[pl.BlockSpec(memory_space=pl.ANY)] * len(shapes),
        scratch_shapes=[
            pltpu.VMEM((TR, H), F32),
            pltpu.VMEM((2, depth, wide), F32),
            pltpu.VMEM((depth, H), F32),
            pltpu.VMEM((depth, H), BF16),
            pltpu.VMEM((depth, H), BF16),
            pltpu.VMEM((step_rows, TR), F32),
            pltpu.VMEM((2, step_rows, TC), F32),
            pltpu.VMEM((steps, pairs, piece, TC), F32),
            pltpu.VMEM((steps, pairs, piece, TC), F32),
            pltpu.VMEM((steps, pairs, piece, TC), F32),
            pltpu.VMEM((steps, piece, TC), F32),
            dma((2, chunks)), dma((2, chunks)), dma((2, chunks)), dma((2, chunks)), dma((2, chunks)),
            dma((len(alternate),)), dma((len(alternate),)), dma((len(alternate),)), dma((len(alternate),)),
            dma((steps, pairs)), dma((steps, pairs)), dma((steps, pairs)), dma((steps, pairs)), dma((steps,)),
            dma((shares, pairs)), dma((shares, pairs)), dma((shares, pairs)), dma((shares, pairs)),
            dma, dma, dma((steps,)), dma((steps,)),
            dma((2,)), dma((2,)), dma,
        ],
        compiler_params=pltpu.CompilerParams(
            collective_id=0, has_side_effects=True, vmem_limit_bytes=60 * 2**20
        ),
        name="gather_symmetric",
    )(precision, samples)[0]


def update_kernel(samples_total, block, ids, sym, prec, rows_o, cols_o, new_t, out, res):
    i = pl.program_id(0)
    M, H = sym.shape
    row_id = ids[0] + i * block + lax.broadcasted_iota(jnp.int32, (M, H), 0)
    col_id = ids[1] + lax.broadcasted_iota(jnp.int32, (M, H), 1)
    on_diagonal = row_id == col_id
    held = prec[...]
    inverse = jnp.where(on_diagonal, 1.0 / jnp.where(on_diagonal, held, 1.0), 0.0)
    gradient = sym[...] / (2.0 * samples_total) - inverse
    stepped = held - step_size * gradient
    threshold = step_size * penalty * 0.5 * (rows_o[...] + cols_o[...])
    size = jnp.maximum(jnp.abs(stepped) - threshold, 0.0)
    shrunk = jnp.where(stepped < 0.0, -size, size)
    updated = jnp.where(on_diagonal, stepped, shrunk)
    out[...] = updated
    u_high, u_low = split(updated)
    n_high, n_low = split(new_t[...])
    count = n_high.shape[0]
    pair = dot(jnp.concatenate([n_high, n_low], axis=0), u_high)
    value = pair[:count] + pair[count:] + dot(n_high, u_low)
    diag = jnp.sum(jnp.where(on_diagonal, held, 0.0), axis=0, keepdims=True)
    diag = jnp.broadcast_to(diag, (8, H))

    @pl.when(i == 0)
    def _():
        res[pl.ds(0, count), :] = value
        res[pl.ds(count, 8), :] = diag

    @pl.when(i > 0)
    def _():
        res[pl.ds(0, count), :] += value
        res[pl.ds(count, 8), :] += diag


def updated_and_partial(symmetric, precision, new_rows, orders_rows, orders_cols, ids, half_index, samples_total):
    TR, H = symmetric.shape
    count = new_rows.shape[0]
    block = 256
    return pl.pallas_call(
        functools.partial(update_kernel, samples_total, block),
        out_shape=[jax.ShapeDtypeStruct((TR, H), F32), jax.ShapeDtypeStruct((count + 8, H), F32)],
        grid_spec=pltpu.PrefetchScalarGridSpec(
            num_scalar_prefetch=1,
            grid=(TR // block,),
            in_specs=[
                pl.BlockSpec((block, H), lambda i, ids: (i, 0)),
                pl.BlockSpec((block, H), lambda i, ids: (i, ids[2])),
                pl.BlockSpec((block, 1), lambda i, ids: (i, 0)),
                pl.BlockSpec((1, H), lambda i, ids: (0, 0)),
                pl.BlockSpec((count, block), lambda i, ids: (0, i)),
            ],
            out_specs=[
                pl.BlockSpec((block, H), lambda i, ids: (i, 0)),
                pl.BlockSpec((count + 8, H), lambda i, ids: (0, 0)),
            ],
        ),
        compiler_params=pltpu.CompilerParams(vmem_limit_bytes=56 * 2**20),
        name="update_rows",
    )(ids, symmetric, precision, orders_rows, orders_cols, new_rows)


def residual_kernel(R, part, out, held, got, diags, send, recv, diag_send, diag_recv):
    r, z, p = lax.axis_index("row"), lax.axis_index("col"), lax.axis_index("rep")
    rows = out.shape[0]
    rounds = R.bit_length() - 1

    def flip(bit):
        low = lax.rem(r // bit, 2)
        return r + bit - 2 * bit * low

    barrier = pltpu.get_barrier_semaphore()
    for d in range(1, R):
        where = (lax.rem(r + d, R), z, p)
        pl.semaphore_signal(barrier, inc=1, device_id=where, device_id_type=MESH)
    pl.semaphore_wait(barrier, R - 1)

    def diag_copy(d):
        where = (lax.rem(r + d, R), z, p)
        return pltpu.make_async_remote_copy(
            src_ref=part.at[pl.ds(rows * R, 8)], dst_ref=diags.at[d - 1], send_sem=diag_send.at[d],
            recv_sem=diag_recv.at[d], device_id=where, device_id_type=MESH)

    def exchange(stage, j):
        bit = 1 << stage
        peer = flip(bit)
        block = lax.rem(peer, 2 * bit) + 2 * bit * j
        src = part if stage == 0 else held
        return pltpu.make_async_remote_copy(
            src_ref=src.at[aligned(block * rows, rows, 8)], dst_ref=got.at[stage, j],
            send_sem=send.at[stage, j], recv_sem=recv.at[stage, j],
            device_id=(peer, z, p), device_id_type=MESH)

    count = [R >> (stage + 1) for stage in range(rounds)]
    for stage in range(rounds):
        bit = 1 << stage
        if stage == 0:
            for j in range(count[0]):
                exchange(0, j).start()
            for d in range(1, R):
                diag_copy(d).start()

        def receive(j, stage=stage, bit=bit):
            mine = lax.rem(r, 2 * bit) + 2 * bit * j
            block = aligned(mine * rows, rows, 8)
            exchange(stage, j).wait_recv()
            src = part if stage == 0 else held
            held[block] = src[block] + got[stage, j]

        for j in range(count[stage]):
            receive(j)
        if stage + 1 < rounds:
            for j in range(count[stage + 1]):
                exchange(stage + 1, j).start()
    diag = part[pl.ds(rows * R, 1)]
    for d in range(1, R):
        diag_copy(d).wait_recv()
        diag = diag + diags[d - 1, pl.ds(0, 1)]
    out[...] = held[aligned(r * rows, rows, 8)] / diag
    for stage in range(rounds):
        for j in range(count[stage]):
            exchange(stage, j).wait_send()
    for d in range(1, R):
        diag_copy(d).wait_send()


def residual_sum(part, R):
    total, H = part.shape
    rows = (total - 8) // R
    assert R & (R - 1) == 0
    rounds = R.bit_length() - 1
    dma = pltpu.SemaphoreType.DMA
    return pl.pallas_call(
        functools.partial(residual_kernel, R),
        out_shape=jax.ShapeDtypeStruct((rows, H), F32),
        in_specs=[pl.BlockSpec(memory_space=pltpu.VMEM)],
        out_specs=pl.BlockSpec(memory_space=pltpu.VMEM),
        scratch_shapes=[
            pltpu.VMEM((R * rows, H), F32),
            pltpu.VMEM((rounds, R // 2, rows, H), F32),
            pltpu.VMEM((R - 1, 8, H), F32),
            dma((rounds, R // 2)), dma((rounds, R // 2)), dma((R,)), dma((R,)),
        ],
        compiler_params=pltpu.CompilerParams(
            collective_id=1, has_side_effects=True, vmem_limit_bytes=40 * 2**20
        ),
        name="residual_sum",
    )(part)


def per_device(precision, samples, new_rows, ngram_order):
    R, C, reps = lax.axis_size("row"), lax.axis_size("col"), lax.axis_size("rep")
    r, c, p = lax.axis_index("row"), lax.axis_index("col"), lax.axis_index("rep")
    TR, TC = precision.shape
    H = TC // reps
    assert reps == 2 and TC % TR == 0 and R * TR == C * TC
    symmetric = gathered(precision, samples, R, C)
    orders = ngram_order.astype(F32)
    row_start, col_start = r * TR, c * TC + p * H
    order_rows = lax.dynamic_slice_in_dim(orders, row_start, TR, 0)[:, None]
    order_cols = lax.dynamic_slice_in_dim(orders, col_start, H, 0)[None, :]
    ids = jnp.stack([row_start, col_start, p]).astype(jnp.int32)
    updated, part = updated_and_partial(
        symmetric, precision, new_rows, order_rows, order_cols, ids, p, samples.shape[0] * reps
    )
    return updated, residual_sum(part, R)


def solution(mesh):
    placed = (P("row", "col"), P("rep", "col"), P(None, "row"), P())
    return jax.shard_map(
        per_device,
        mesh=mesh,
        in_specs=placed,
        out_specs=(P("row", ("col", "rep")), P("row", ("col", "rep"))),
        check_vma=False,
    )
```

```python
import functools

import jax
import jax.numpy as jnp
from jax import lax
from jax.experimental import pallas as pl
from jax.experimental.pallas import tpu as pltpu
from jax.sharding import PartitionSpec as P

step_size = 0.25
penalty = 0.08
MESH = pl.DeviceIdType.MESH
F32 = jnp.float32
BF16 = jnp.bfloat16
step_rows = 256
chunk_rows = 64
depth = 256
alternate = ((0, 3), (0, 7))


def block_of(size, most=512):
    for block in (1024, 768, 512, 384, 256, 128):
        if block <= most and size % block == 0:
            return block
    return size


def split(values):
    high = values.astype(BF16)
    return high, (values - high.astype(F32)).astype(BF16)


def dot(left, right):
    return jnp.dot(left, right, preferred_element_type=F32)


def aligned(start, size, unit):
    return pl.ds(pl.multiple_of(start, unit), size)


def gather_kernel(
    R, C, S, TR, TC, H,
    prec, samp,
    acc_out, x_near, x_far, y_near, y_far, y_cols, x_cols_far, y_cols_far, kept_rows,
    acc, left, right, right_high, right_low, x_rows, partial, paired, mid, arrived, reduced,
    up_send, down_send, side_send, near_recv, far_recv, alt_up, alt_down, alt_over, alt_recv,
    pair_send, pair_recv, rs_send, rs_recv, own_copy,
    share_send, share_recv, hand_send, hand_recv,
    xq_send, xq_recv, yq_send, yq_recv,
    om_sem, load_sem, out_sem,
):
    r, z, p = lax.axis_index("row"), lax.axis_index("col"), lax.axis_index("rep")
    ratio = TC // TR
    other = 1 - p
    source = r // ratio
    offset = (r % ratio) * TR
    is_source = z == source
    has_up = jnp.logical_and(z >= source, z < C - 1)
    has_down = jnp.logical_and(z <= source, z > 0)
    alt = lax.rem(r + R // 2, R)
    alt_source = alt // ratio
    is_alt_source = z == alt_source
    alt_has_up = jnp.logical_and(z >= alt_source, z < C - 1)
    alt_has_down = jnp.logical_and(z <= alt_source, z > 0)
    alt_cols = aligned((alt % ratio) * TR, TR, 128)
    steps = S // step_rows
    chunks = S // chunk_rows
    per_step = step_rows // chunk_rows
    piece = step_rows // R
    quarter = S // R
    own_cols = aligned(p * H, H, 128)
    far_cols = aligned(other * H, H, 128)
    tile_cols = aligned(offset, TR, 128)

    pairs = R // 2
    twin = r + 1 - 2 * lax.rem(r, 2)
    parity = lax.rem(r, 2)
    group_index = r // 2

    def mate(d):
        return lax.rem(r + d, R)

    def peer(e):
        return lax.rem(r + 2 * e, R)

    def sender_of(e):
        return lax.rem(r + R - 2 * e, R)

    def remote(src, dst, send, recv, where):
        return pltpu.make_async_remote_copy(
            src_ref=src, dst_ref=dst, send_sem=send, recv_sem=recv, device_id=where, device_id_type=MESH
        )

    across = (r, z, other)

    barrier = pltpu.get_barrier_semaphore()
    pl.semaphore_signal(barrier, inc=1, device_id=across, device_id_type=MESH)
    for d in range(1, R):
        pl.semaphore_signal(barrier, inc=1, device_id=(mate(d), z, p), device_id_type=MESH)

    for hop in (1, C - 1):
        pl.semaphore_signal(barrier, inc=1, device_id=(r, lax.rem(z + hop, C), p), device_id_type=MESH)
    pl.semaphore_wait(barrier, R + 2)

    kinds = ((samp, x_near, x_far), (y_cols, y_near, y_far))

    def near_copies(kind, i, wide):
        wide_ref, near, far = kinds[kind]
        rows = aligned(i * chunk_rows, chunk_rows, chunk_rows)
        src = wide_ref.at[rows, tile_cols] if wide else near.at[rows]
        up = remote(src, near.at[rows], up_send.at[kind, i], near_recv.at[kind, i], (r, z + 1, p))
        down = remote(src, near.at[rows], down_send.at[kind, i], near_recv.at[kind, i], (r, z - 1, p))
        side = remote(src, far.at[rows], side_send.at[kind, i], far_recv.at[kind, i], across)
        return up, down, side

    def pass_on(kind, i, wide):
        up, down, side = near_copies(kind, i, wide)

        @pl.when(has_up)
        def _():
            up.start()

        @pl.when(has_down)
        def _():
            down.start()

        side.start()

    def alt_copies(kind, i, wide):
        wide_ref, near, _ = kinds[kind]
        j = alternate.index((kind, i))
        rows = aligned(i * chunk_rows, chunk_rows, chunk_rows)
        kept = kept_rows.at[pl.ds(j * chunk_rows, chunk_rows)]
        src = wide_ref.at[rows, alt_cols] if wide else kept
        up = remote(src, kept, alt_up.at[j], alt_recv.at[j], (r, z + 1, p))
        down = remote(src, kept, alt_down.at[j], alt_recv.at[j], (r, z - 1, p))
        over = remote(kept, near.at[rows], alt_over.at[j], near_recv.at[kind, i], (alt, z, p))
        return up, down, over

    def pass_alt(kind, i, wide):
        up, down, _ = alt_copies(kind, i, wide)

        @pl.when(alt_has_up)
        def _():
            up.start()

        @pl.when(alt_has_down)
        def _():
            down.start()

    def start_source(kind, i):
        @pl.when(is_source)
        def _():
            if (kind, i) in alternate:
                near_copies(kind, i, True)[2].start()
            else:
                pass_on(kind, i, True)

        if (kind, i) in alternate:
            @pl.when(is_alt_source)
            def _():
                pass_alt(kind, i, True)

    def serve(kind, i):
        if (kind, i) in alternate:
            @pl.when(jnp.logical_not(is_alt_source))
            def _():
                alt_copies(kind, i, False)[0].wait_recv()
                pass_alt(kind, i, False)
                alt_copies(kind, i, False)[2].start()

        @pl.when(jnp.logical_not(is_source))
        def _():
            near_copies(kind, i, False)[0].wait_recv()
            if (kind, i) in alternate:
                near_copies(kind, i, False)[2].start()
            else:
                pass_on(kind, i, False)

    def wait_far(kind, i):
        near_copies(kind, i, False)[2].wait_recv()

    def wait_sent(kind, i):
        up, down, side = near_copies(kind, i, False)
        side.wait_send()
        if (kind, i) in alternate:
            up, down, over = alt_copies(kind, i, False)

            @pl.when(jnp.logical_not(is_alt_source))
            def _():
                over.wait_send()

        rises, falls = (alt_has_up, alt_has_down) if (kind, i) in alternate else (has_up, has_down)

        @pl.when(rises)
        def _():
            up.wait_send()

        @pl.when(falls)
        def _():
            down.wait_send()

    def xq_copy():
        rows = aligned(r * quarter, quarter, 8)
        return remote(samp.at[rows, far_cols], x_cols_far.at[rows], xq_send, xq_recv, across)

    def step_piece(s, owner):
        return aligned(s * step_rows + owner * piece, piece, 8)

    def pair_copy(s, slot, j):
        rows = aligned((2 * j + 1 - parity) * piece, piece, 8)
        return remote(
            partial.at[slot, rows], paired.at[s, j], pair_send.at[s, j], pair_recv.at[s, j], (twin, z, p)
        )

    def rs_copy(s, e):
        return remote(
            mid.at[s, peer(e) // 2], arrived.at[s, e - 1], rs_send.at[s, e], rs_recv.at[s, e], (peer(e), z, p)
        )

    def own_piece(s):
        return pltpu.make_async_copy(reduced.at[s], y_cols.at[step_piece(s, r)], own_copy.at[s])

    def yq_copy(s):
        return remote(
            reduced.at[s, :, far_cols], y_cols_far.at[step_piece(s, r)], yq_send.at[s], yq_recv.at[s], across
        )

    def shared(which, owner):
        if which == 2 * steps:
            return x_cols_far.at[aligned(owner * quarter, quarter, 8)]
        if which < steps:
            return y_cols.at[step_piece(which, owner)]
        return y_cols_far.at[step_piece(which - steps, owner)]

    def share_copy(which, e, owner, src=None):
        piece_ref = shared(which, owner)
        return remote(
            piece_ref if src is None else src, piece_ref,
            share_send.at[which, e], share_recv.at[which, e], (peer(e), z, p),
        )

    def hand_copy(which, owner, src=None):
        piece_ref = shared(which, owner)
        g = owner // 2
        return remote(
            piece_ref if src is None else src, piece_ref,
            hand_send.at[which, g], hand_recv.at[which, g], (twin, z, p),
        )

    def share(which, src=None):
        for e in range(1, pairs):
            share_copy(which, e, r, src).start()
        hand_copy(which, r, src).start()

    def hand_on(which):
        for e in range(1, pairs):
            owner = sender_of(e)
            share_copy(which, e, owner).wait_recv()
            hand_copy(which, owner).start()

    def wait_handed(which):
        for g in range(pairs):
            hand_copy(which, 2 * g + 1 - parity).wait_recv()

    def wait_shared(which):
        for e in range(1, pairs):
            share_copy(which, e, r).wait_send()
        for g in range(pairs):
            hand_copy(which, 2 * g + parity).wait_send()

    for i in range(chunks):
        start_source(0, i)
    xq_copy().start()

    def om_copy(b, slot):
        rows = aligned(b * depth, depth, depth)
        return pltpu.make_async_copy(prec.at[rows], left.at[slot, :, pl.ds(0, TC)], om_sem.at[slot])

    blocks = TR // depth
    wide_block = block_of(TC, 1024)

    def combine(s, slot):
        for j in range(pairs):
            pair_copy(s, slot, j).wait_recv()
            rows = aligned((2 * j + parity) * piece, piece, 8)
            mid[s, j] = partial[slot, rows] + paired[s, j]
        for e in range(1, pairs):
            rs_copy(s, e).start()

    def finish(s):
        total = mid[s, group_index]
        for e in range(1, pairs):
            rs_copy(s, e).wait_recv()
            total = total + arrived[s, e - 1]
        reduced[s] = total
        own_piece(s).start()
        share(s, reduced.at[s])
        yq_copy(s).start()

    def source_step(s):
        own_piece(s).wait()
        wait_handed(s)
        for j in range(per_step):
            start_source(1, s * per_step + j)

    def spread_far(s):
        yq_copy(s).wait_recv()
        share(steps + s)

    def load_x(s):
        rows = aligned(s * step_rows, step_rows, step_rows)

        @pl.when(is_source)
        def _():
            pltpu.make_async_copy(samp.at[rows, tile_cols], x_rows, load_sem.at[0]).start()

        @pl.when(jnp.logical_not(is_source))
        def _():
            pltpu.make_async_copy(x_near.at[rows], x_rows, load_sem.at[0]).start()

        pltpu.make_async_copy(x_near.at[rows], x_rows, load_sem.at[0]).wait()

    def products_step(slot):
        @pl.loop(0, blocks)
        def _(b):
            here = lax.rem(b, 2)
            om_copy(b, here).wait()

            @pl.when(b + 1 < blocks)
            def _():
                om_copy(b + 1, 1 - here).start()

            high, low = split(x_rows[:, aligned(b * depth, depth, depth)])
            both = jnp.concatenate([high, low], axis=0)
            for n in range(TC // wide_block):
                cols = pl.ds(n * wide_block, wide_block)
                w_high, w_low = split(left[here, :, cols])
                pair = dot(both, w_high)
                value = pair[:step_rows] + pair[step_rows:] + dot(high, w_low)

                @pl.when(b == 0)
                def _():
                    partial[slot, :, cols] = value

                @pl.when(b > 0)
                def _():
                    partial[slot, :, cols] += value

    def products(s):
        load_x(s)
        if s >= 2:
            for j in range(pairs):
                pair_copy(s - 2, s % 2, j).wait_send()
        products_step(s % 2)
        for j in range(pairs):
            pair_copy(s, s % 2, j).start()
        if s + 1 < steps:
            om_copy(0, 0).start()

    def serve_x(i):
        serve(0, i)

    def serve_y(i):
        serve(1, i)

    def mix(s):
        combine(s, s % 2)

    def spread_x(_):
        xq_copy().wait_recv()
        share(2 * steps)

    def hand_far(s):
        hand_on(steps + s)

    assert steps == 2 and chunks == 8
    om_copy(0, 0).start()
    order = (
        (serve_x, 0), (serve_x, 1), (serve_x, 2), (serve_x, 3), (products, 0), (serve_x, 6), (serve_x, 7),
        (mix, 0), (finish, 0), (serve_x, 5), (hand_on, 0), (serve_x, 4), (source_step, 0), (products, 1),
        (mix, 1), (serve_y, 1), (serve_y, 0), (finish, 1), (spread_x, 0),
    )
    for action, index in order:
        action(index)
    terms = (0, 1, 4, 2, 5, 3, 6, 7)
    between = {
        1: (
            (hand_on, 1), (serve_y, 2), (serve_y, 3), (spread_far, 0), (source_step, 1), (spread_far, 1),
        ),
        3: (
            (hand_far, 0), (hand_far, 1), (hand_on, 2 * steps), (serve_y, 5), (serve_y, 6),
        ),
        5: (
            (serve_y, 4),
        ),
        6: (
            (serve_y, 7),
        ),
    }

    m_block, n_block = block_of(TR), block_of(H)
    out_blocks = TR // m_block
    halves = S // depth
    group = depth // chunk_rows

    def out_copy(i):
        rows = aligned(i * m_block, m_block, m_block)
        return pltpu.make_async_copy(acc.at[rows], acc_out.at[rows], out_sem)

    def load(src_left, src_right):
        pltpu.make_async_copy(src_left, left.at[0, :, pl.ds(0, TR)], load_sem.at[0]).start()
        pltpu.make_async_copy(src_right, right, load_sem.at[1]).start()

    def near_ref(kind, rows):
        def run(src_right):
            @pl.when(is_source)
            def _():
                load(kinds[kind][0].at[rows, tile_cols], src_right)

            @pl.when(jnp.logical_not(is_source))
            def _():
                load(kinds[kind][1].at[rows], src_right)

        return run

    def begin(place):
        u = terms[place]
        for action, index in between.get(place, ()):
            action(index)
        if u in (2, 3):
            for s in range(steps // 2):
                wait_handed(steps + (u - 2) * (steps // 2) + s)
        if u in (5, 7) and not {5, 7} & set(terms[:place]):
            wait_handed(2 * steps)
        if u in (2, 3):
            for i in range(group):
                wait_far(0, (u - 2) * group + i)
        if u in (5, 7):
            for i in range(group):
                wait_far(1, (u - 5) // 2 * group + i)
        k = u % 2 if u < 4 else (u - 4) // 2
        rows = pl.ds(k * depth, depth)
        if u < 2:
            near_ref(0, rows)(y_cols.at[rows, own_cols])
        elif u < 4:
            load(x_far.at[rows], y_cols_far.at[rows])
        elif u % 2 == 0:
            near_ref(1, rows)(samp.at[rows, own_cols])
        else:
            load(y_far.at[rows], x_cols_far.at[rows])

    assert halves == 2

    @pl.loop(0, 8)
    def _(u):
        for case in range(8):
            @pl.when(u == case)
            def _(case=case):
                begin(case)

        pltpu.make_async_copy(x_far.at[pl.ds(0, depth)], left.at[0, :, pl.ds(0, TR)], load_sem.at[0]).wait()
        pltpu.make_async_copy(y_cols_far.at[pl.ds(0, depth)], right, load_sem.at[1]).wait()
        high, low = split(right[...])
        right_high[...] = high
        right_low[...] = low

        @pl.loop(0, out_blocks)
        def _(i):
            rows = aligned(i * m_block, m_block, m_block)
            l_high, l_low = split(left[0, :, rows].T)
            for n in range(H // n_block):
                cols = pl.ds(n * n_block, n_block)
                value = dot(l_high, right_high[:, cols]) + dot(l_low, right_high[:, cols])
                value = value + dot(l_high, right_low[:, cols])

                @pl.when(u == 0)
                def _():
                    acc[rows, cols] = value

                @pl.when(u > 0)
                def _():
                    acc[rows, cols] += value

            @pl.when(u == 7)
            def _():
                out_copy(i).start()

    for i in range(chunks):
        wait_sent(0, i)
        wait_sent(1, i)

    xq_copy().wait_send()
    for which in range(2 * steps + 1):
        wait_shared(which)
    for s in range(steps):
        yq_copy(s).wait_send()
        for e in range(1, pairs):
            rs_copy(s, e).wait_send()
        if s >= steps - 2:
            for j in range(pairs):
                pair_copy(s, s % 2, j).wait_send()

    @pl.loop(0, out_blocks)
    def _(i):
        out_copy(i).wait()


def gathered(precision, samples, R, C):
    TR, TC = precision.shape
    S = samples.shape[0]
    H = TC // 2
    assert C > 2
    steps, chunks = S // step_rows, S // chunk_rows
    piece = step_rows // R
    pairs, shares = R // 2, 2 * steps + 1
    assert R % 2 == 0
    wide = max(TR, TC)
    dma = pltpu.SemaphoreType.DMA
    shapes = [(TR, H), (S, TR), (S, TR), (S, TR), (S, TR), (S, TC), (S, H), (S, H)]
    shapes.append((len(alternate) * chunk_rows, TR))
    return pl.pallas_call(
        functools.partial(gather_kernel, R, C, S, TR, TC, H),
        out_shape=[jax.ShapeDtypeStruct(shape, F32) for shape in shapes],
        in_specs=[pl.BlockSpec(memory_space=pl.ANY)] * 2,
        out_specs=[pl.BlockSpec(memory_space=pl.ANY)] * len(shapes),
        scratch_shapes=[
            pltpu.VMEM((TR, H), F32),
            pltpu.VMEM((2, depth, wide), F32),
            pltpu.VMEM((depth, H), F32),
            pltpu.VMEM((depth, H), BF16),
            pltpu.VMEM((depth, H), BF16),
            pltpu.VMEM((step_rows, TR), F32),
            pltpu.VMEM((2, step_rows, TC), F32),
            pltpu.VMEM((steps, pairs, piece, TC), F32),
            pltpu.VMEM((steps, pairs, piece, TC), F32),
            pltpu.VMEM((steps, pairs, piece, TC), F32),
            pltpu.VMEM((steps, piece, TC), F32),
            dma((2, chunks)), dma((2, chunks)), dma((2, chunks)), dma((2, chunks)), dma((2, chunks)),
            dma((len(alternate),)), dma((len(alternate),)), dma((len(alternate),)), dma((len(alternate),)),
            dma((steps, pairs)), dma((steps, pairs)), dma((steps, pairs)), dma((steps, pairs)), dma((steps,)),
            dma((shares, pairs)), dma((shares, pairs)), dma((shares, pairs)), dma((shares, pairs)),
            dma, dma, dma((steps,)), dma((steps,)),
            dma((2,)), dma((2,)), dma,
        ],
        compiler_params=pltpu.CompilerParams(
            collective_id=0, has_side_effects=True, vmem_limit_bytes=60 * 2**20
        ),
        name="gather_symmetric",
    )(precision, samples)[0]


def update_kernel(samples_total, block, ids, sym, prec, rows_o, cols_o, new_t, out, res):
    i = pl.program_id(0)
    M, H = sym.shape
    count = new_t.shape[0]

    @pl.when(i == 0)
    def _():
        res[...] = jnp.zeros_like(res)

    n_high, n_low = split(new_t[...])
    both = jnp.concatenate([n_high, n_low], axis=0)
    wide = block_of(H)
    row_id = ids[0] + i * block + lax.broadcasted_iota(jnp.int32, (M, wide), 0)
    order_rows = rows_o[...].T[:, :1]
    for n in range(H // wide):
        cols = pl.ds(n * wide, wide)
        col_id = ids[1] + n * wide + lax.broadcasted_iota(jnp.int32, (M, wide), 1)
        on_diagonal = row_id == col_id
        held = prec[:, cols]
        diag = jnp.sum(jnp.where(on_diagonal, held, 0.0), axis=0, keepdims=True)
        inverse = jnp.where(on_diagonal, 1.0 / diag, 0.0)
        gradient = sym[:, cols] / (2.0 * samples_total) - inverse
        stepped = held - step_size * gradient
        threshold = step_size * penalty * 0.5 * (order_rows + cols_o[:, cols])
        size = jnp.maximum(jnp.abs(stepped) - threshold, 0.0)
        shrunk = jnp.where(stepped < 0.0, -size, size)
        updated = jnp.where(on_diagonal, stepped, shrunk)
        out[:, cols] = updated
        u_high, u_low = split(updated)
        pair = dot(both, u_high)
        value = pair[:count] + pair[count:] + dot(n_high, u_low)
        res[pl.ds(0, count), cols] += value
        res[pl.ds(count, 8), cols] += jnp.broadcast_to(diag, (8, wide))


def updated_and_partial(symmetric, precision, new_rows, orders_rows, orders_cols, ids, half_index, samples_total):
    TR, H = symmetric.shape
    count = new_rows.shape[0]
    block = 256

    return pl.pallas_call(
        functools.partial(update_kernel, samples_total, block),
        out_shape=[jax.ShapeDtypeStruct((TR, H), F32), jax.ShapeDtypeStruct((count + 8, H), F32)],
        grid_spec=pltpu.PrefetchScalarGridSpec(
            num_scalar_prefetch=1,
            grid=(TR // block,),
            in_specs=[
                pl.BlockSpec((block, H), lambda i, ids: (i, 0)),
                pl.BlockSpec((block, H), lambda i, ids: (i, ids[2])),
                pl.BlockSpec((8, block), lambda i, ids: (0, i)),
                pl.BlockSpec((1, H), lambda i, ids: (0, 0)),
                pl.BlockSpec((count, block), lambda i, ids: (0, i)),
            ],
            out_specs=[
                pl.BlockSpec((block, H), lambda i, ids: (i, 0)),
                pl.BlockSpec((count + 8, H), lambda i, ids: (0, 0)),
            ],
        ),
        compiler_params=pltpu.CompilerParams(vmem_limit_bytes=56 * 2**20),
        name="update_rows",
    )(ids, symmetric, precision, orders_rows, orders_cols, new_rows)


def residual_kernel(R, part, out, held, got, diags, send, recv, diag_send, diag_recv):
    r, z, p = lax.axis_index("row"), lax.axis_index("col"), lax.axis_index("rep")
    rows = out.shape[0]
    rounds = R.bit_length() - 1

    def flip(bit):
        low = lax.rem(r // bit, 2)
        return r + bit - 2 * bit * low

    barrier = pltpu.get_barrier_semaphore()
    for d in range(1, R):
        where = (lax.rem(r + d, R), z, p)
        pl.semaphore_signal(barrier, inc=1, device_id=where, device_id_type=MESH)
    pl.semaphore_wait(barrier, R - 1)

    def diag_copy(d):
        where = (lax.rem(r + d, R), z, p)
        return pltpu.make_async_remote_copy(
            src_ref=part.at[pl.ds(rows * R, 8)], dst_ref=diags.at[d - 1], send_sem=diag_send.at[d],
            recv_sem=diag_recv.at[d], device_id=where, device_id_type=MESH)

    def exchange(stage, j):
        bit = 1 << stage
        peer = flip(bit)
        block = lax.rem(peer, 2 * bit) + 2 * bit * j
        src = part if stage == 0 else held
        return pltpu.make_async_remote_copy(
            src_ref=src.at[aligned(block * rows, rows, 8)], dst_ref=got.at[stage, j],
            send_sem=send.at[stage, j], recv_sem=recv.at[stage, j],
            device_id=(peer, z, p), device_id_type=MESH)

    count = [R >> (stage + 1) for stage in range(rounds)]
    for stage in range(rounds):
        bit = 1 << stage
        if stage == 0:
            for j in range(count[0]):
                exchange(0, j).start()
            for d in range(1, R):
                diag_copy(d).start()

        def receive(j, stage=stage, bit=bit):
            mine = lax.rem(r, 2 * bit) + 2 * bit * j
            block = aligned(mine * rows, rows, 8)
            exchange(stage, j).wait_recv()
            src = part if stage == 0 else held
            held[block] = src[block] + got[stage, j]

        for j in range(count[stage]):
            receive(j)
        if stage + 1 < rounds:
            for j in range(count[stage + 1]):
                exchange(stage + 1, j).start()
    diag = part[pl.ds(rows * R, 1)]
    for d in range(1, R):
        diag_copy(d).wait_recv()
        diag = diag + diags[d - 1, pl.ds(0, 1)]
    out[...] = held[aligned(r * rows, rows, 8)] / diag
    for stage in range(rounds):
        for j in range(count[stage]):
            exchange(stage, j).wait_send()
    for d in range(1, R):
        diag_copy(d).wait_send()


def residual_sum(part, R):
    total, H = part.shape
    rows = (total - 8) // R
    assert R & (R - 1) == 0
    rounds = R.bit_length() - 1
    dma = pltpu.SemaphoreType.DMA
    return pl.pallas_call(
        functools.partial(residual_kernel, R),
        out_shape=jax.ShapeDtypeStruct((rows, H), F32),
        in_specs=[pl.BlockSpec(memory_space=pltpu.VMEM)],
        out_specs=pl.BlockSpec(memory_space=pltpu.VMEM),
        scratch_shapes=[
            pltpu.VMEM((R * rows, H), F32),
            pltpu.VMEM((rounds, R // 2, rows, H), F32),
            pltpu.VMEM((R - 1, 8, H), F32),
            dma((rounds, R // 2)), dma((rounds, R // 2)), dma((R,)), dma((R,)),
        ],
        compiler_params=pltpu.CompilerParams(
            collective_id=1, has_side_effects=True, vmem_limit_bytes=40 * 2**20
        ),
        name="residual_sum",
    )(part)


def per_device(precision, samples, new_rows, ngram_order):
    R, C, reps = lax.axis_size("row"), lax.axis_size("col"), lax.axis_size("rep")
    r, c, p = lax.axis_index("row"), lax.axis_index("col"), lax.axis_index("rep")
    TR, TC = precision.shape
    H = TC // reps
    assert reps == 2 and TC % TR == 0 and R * TR == C * TC
    symmetric = gathered(precision, samples, R, C)
    orders = ngram_order.astype(F32)
    row_start, col_start = r * TR, c * TC + p * H
    order_rows = jnp.broadcast_to(lax.dynamic_slice_in_dim(orders, row_start, TR, 0)[None, :], (8, TR))
    order_cols = lax.dynamic_slice_in_dim(orders, col_start, H, 0)[None, :]
    ids = jnp.stack([row_start, col_start, p]).astype(jnp.int32)
    updated, part = updated_and_partial(
        symmetric, precision, new_rows, order_rows, order_cols, ids, p, samples.shape[0] * reps
    )
    return updated, residual_sum(part, R)


def solution(mesh):
    placed = (P("row", "col"), P("rep", "col"), P(None, "row"), P())
    return jax.shard_map(
        per_device,
        mesh=mesh,
        in_specs=placed,
        out_specs=(P("row", ("col", "rep")), P("row", ("col", "rep"))),
        check_vma=False,
    )
```

```python
import functools

import jax
import jax.numpy as jnp
from jax import lax
from jax.experimental import pallas as pl
from jax.experimental.pallas import tpu as pltpu
from jax.sharding import PartitionSpec as P

step_size = 0.25
penalty = 0.08
MESH = pl.DeviceIdType.MESH
F32 = jnp.float32
BF16 = jnp.bfloat16
step_rows = 256
chunk_rows = 64
depth = 256
alternate = ((0, 3), (0, 7))


def block_of(size, most=512):
    for block in (1024, 768, 512, 384, 256, 128):
        if block <= most and size % block == 0:
            return block
    return size


def split(values):
    high = values.astype(BF16)
    return high, (values - high.astype(F32)).astype(BF16)


def dot(left, right):
    return jnp.dot(left, right, preferred_element_type=F32)


def aligned(start, size, unit):
    return pl.ds(pl.multiple_of(start, unit), size)


def gather_kernel(
    R, C, S, TR, TC, H,
    prec, samp,
    acc_out, x_near, x_far, y_near, y_far, y_cols, x_cols_far, y_cols_far, kept_rows,
    acc, left, right, right_high, right_low, x_rows, partial, paired, mid, arrived, reduced,
    up_send, down_send, side_send, near_recv, far_recv, alt_up, alt_down, alt_over, alt_recv,
    pair_send, pair_recv, rs_send, rs_recv, own_copy,
    share_send, share_recv, hand_send, hand_recv,
    xq_send, xq_recv, yq_send, yq_recv,
    om_sem, load_sem, out_sem,
):
    r, z, p = lax.axis_index("row"), lax.axis_index("col"), lax.axis_index("rep")
    ratio = TC // TR
    other = 1 - p
    source = r // ratio
    offset = (r % ratio) * TR
    is_source = z == source
    has_up = jnp.logical_and(z >= source, z < C - 1)
    has_down = jnp.logical_and(z <= source, z > 0)
    alt = lax.rem(r + R // 2, R)
    alt_source = alt // ratio
    is_alt_source = z == alt_source
    alt_has_up = jnp.logical_and(z >= alt_source, z < C - 1)
    alt_has_down = jnp.logical_and(z <= alt_source, z > 0)
    alt_cols = aligned((alt % ratio) * TR, TR, 128)
    steps = S // step_rows
    chunks = S // chunk_rows
    per_step = step_rows // chunk_rows
    piece = step_rows // R
    quarter = S // R
    own_cols = aligned(p * H, H, 128)
    far_cols = aligned(other * H, H, 128)
    tile_cols = aligned(offset, TR, 128)

    pairs = R // 2
    twin = r + 1 - 2 * lax.rem(r, 2)
    parity = lax.rem(r, 2)
    group_index = r // 2

    def mate(d):
        return lax.rem(r + d, R)

    def peer(e):
        return lax.rem(r + 2 * e, R)

    def sender_of(e):
        return lax.rem(r + R - 2 * e, R)

    def remote(src, dst, send, recv, where):
        return pltpu.make_async_remote_copy(
            src_ref=src, dst_ref=dst, send_sem=send, recv_sem=recv, device_id=where, device_id_type=MESH
        )

    across = (r, z, other)

    barrier = pltpu.get_barrier_semaphore()
    pl.semaphore_signal(barrier, inc=1, device_id=across, device_id_type=MESH)
    for d in range(1, R):
        pl.semaphore_signal(barrier, inc=1, device_id=(mate(d), z, p), device_id_type=MESH)

    for hop in (1, C - 1):
        pl.semaphore_signal(barrier, inc=1, device_id=(r, lax.rem(z + hop, C), p), device_id_type=MESH)
    pl.semaphore_wait(barrier, R + 2)

    kinds = ((samp, x_near, x_far), (y_cols, y_near, y_far))

    def near_copies(kind, i, wide):
        wide_ref, near, far = kinds[kind]
        rows = aligned(i * chunk_rows, chunk_rows, chunk_rows)
        src = wide_ref.at[rows, tile_cols] if wide else near.at[rows]
        up = remote(src, near.at[rows], up_send.at[kind, i], near_recv.at[kind, i], (r, z + 1, p))
        down = remote(src, near.at[rows], down_send.at[kind, i], near_recv.at[kind, i], (r, z - 1, p))
        side = remote(src, far.at[rows], side_send.at[kind, i], far_recv.at[kind, i], across)
        return up, down, side

    def pass_on(kind, i, wide):
        up, down, side = near_copies(kind, i, wide)

        @pl.when(has_up)
        def _():
            up.start()

        @pl.when(has_down)
        def _():
            down.start()

        side.start()

    def alt_copies(kind, i, wide):
        wide_ref, near, _ = kinds[kind]
        j = alternate.index((kind, i))
        rows = aligned(i * chunk_rows, chunk_rows, chunk_rows)
        kept = kept_rows.at[pl.ds(j * chunk_rows, chunk_rows)]
        src = wide_ref.at[rows, alt_cols] if wide else kept
        up = remote(src, kept, alt_up.at[j], alt_recv.at[j], (r, z + 1, p))
        down = remote(src, kept, alt_down.at[j], alt_recv.at[j], (r, z - 1, p))
        over = remote(kept, near.at[rows], alt_over.at[j], near_recv.at[kind, i], (alt, z, p))
        return up, down, over

    def pass_alt(kind, i, wide):
        up, down, _ = alt_copies(kind, i, wide)

        @pl.when(alt_has_up)
        def _():
            up.start()

        @pl.when(alt_has_down)
        def _():
            down.start()

    def start_source(kind, i):
        @pl.when(is_source)
        def _():
            if (kind, i) in alternate:
                near_copies(kind, i, True)[2].start()
            else:
                pass_on(kind, i, True)

        if (kind, i) in alternate:
            @pl.when(is_alt_source)
            def _():
                pass_alt(kind, i, True)

    def serve(kind, i):
        if (kind, i) in alternate:
            @pl.when(jnp.logical_not(is_alt_source))
            def _():
                alt_copies(kind, i, False)[0].wait_recv()
                pass_alt(kind, i, False)
                alt_copies(kind, i, False)[2].start()

        @pl.when(jnp.logical_not(is_source))
        def _():
            near_copies(kind, i, False)[0].wait_recv()
            if (kind, i) in alternate:
                near_copies(kind, i, False)[2].start()
            else:
                pass_on(kind, i, False)

    def wait_far(kind, i):
        near_copies(kind, i, False)[2].wait_recv()

    def wait_sent(kind, i):
        up, down, side = near_copies(kind, i, False)
        side.wait_send()
        if (kind, i) in alternate:
            up, down, over = alt_copies(kind, i, False)

            @pl.when(jnp.logical_not(is_alt_source))
            def _():
                over.wait_send()

        rises, falls = (alt_has_up, alt_has_down) if (kind, i) in alternate else (has_up, has_down)

        @pl.when(rises)
        def _():
            up.wait_send()

        @pl.when(falls)
        def _():
            down.wait_send()

    def xq_copy():
        rows = aligned(r * quarter, quarter, 8)
        return remote(samp.at[rows, far_cols], x_cols_far.at[rows], xq_send, xq_recv, across)

    def step_piece(s, owner):
        return aligned(s * step_rows + owner * piece, piece, 8)

    def pair_copy(s, slot, j):
        rows = aligned((2 * j + 1 - parity) * piece, piece, 8)
        return remote(
            partial.at[slot, rows], paired.at[s, j], pair_send.at[s, j], pair_recv.at[s, j], (twin, z, p)
        )

    def rs_copy(s, e):
        return remote(
            mid.at[s, peer(e) // 2], arrived.at[s, e - 1], rs_send.at[s, e], rs_recv.at[s, e], (peer(e), z, p)
        )

    def own_piece(s):
        return pltpu.make_async_copy(reduced.at[s], y_cols.at[step_piece(s, r)], own_copy.at[s])

    def yq_copy(s):
        return remote(
            reduced.at[s, :, far_cols], y_cols_far.at[step_piece(s, r)], yq_send.at[s], yq_recv.at[s], across
        )

    def shared(which, owner):
        if which == 2 * steps:
            return x_cols_far.at[aligned(owner * quarter, quarter, 8)]
        if which < steps:
            return y_cols.at[step_piece(which, owner)]
        return y_cols_far.at[step_piece(which - steps, owner)]

    def share_copy(which, e, owner, src=None):
        piece_ref = shared(which, owner)
        return remote(
            piece_ref if src is None else src, piece_ref,
            share_send.at[which, e], share_recv.at[which, e], (peer(e), z, p),
        )

    def hand_copy(which, owner, src=None):
        piece_ref = shared(which, owner)
        g = owner // 2
        return remote(
            piece_ref if src is None else src, piece_ref,
            hand_send.at[which, g], hand_recv.at[which, g], (twin, z, p),
        )

    def share(which, src=None):
        for e in range(1, pairs):
            share_copy(which, e, r, src).start()
        hand_copy(which, r, src).start()

    def hand_on(which):
        for e in range(1, pairs):
            owner = sender_of(e)
            share_copy(which, e, owner).wait_recv()
            hand_copy(which, owner).start()

    def wait_handed(which):
        for g in range(pairs):
            hand_copy(which, 2 * g + 1 - parity).wait_recv()

    def wait_shared(which):
        for e in range(1, pairs):
            share_copy(which, e, r).wait_send()
        for g in range(pairs):
            hand_copy(which, 2 * g + parity).wait_send()

    for i in range(chunks):
        start_source(0, i)
    xq_copy().start()

    def om_copy(b, slot):
        rows = aligned(b * depth, depth, depth)
        return pltpu.make_async_copy(prec.at[rows], left.at[slot, :, pl.ds(0, TC)], om_sem.at[slot])

    blocks = TR // depth
    wide_block = block_of(TC, 1024)

    def combine(s, slot):
        for j in range(pairs):
            pair_copy(s, slot, j).wait_recv()
            rows = aligned((2 * j + parity) * piece, piece, 8)
            mid[s, j] = partial[slot, rows] + paired[s, j]
        for e in range(1, pairs):
            rs_copy(s, e).start()

    def finish(s):
        total = mid[s, group_index]
        for e in range(1, pairs):
            rs_copy(s, e).wait_recv()
            total = total + arrived[s, e - 1]
        reduced[s] = total
        own_piece(s).start()
        share(s, reduced.at[s])
        yq_copy(s).start()

    def source_step(s):
        own_piece(s).wait()
        wait_handed(s)
        for j in range(per_step):
            start_source(1, s * per_step + j)

    def spread_far(s):
        yq_copy(s).wait_recv()
        share(steps + s)

    def load_x(s):
        rows = aligned(s * step_rows, step_rows, step_rows)

        @pl.when(is_source)
        def _():
            pltpu.make_async_copy(samp.at[rows, tile_cols], x_rows, load_sem.at[0]).start()

        @pl.when(jnp.logical_not(is_source))
        def _():
            pltpu.make_async_copy(x_near.at[rows], x_rows, load_sem.at[0]).start()

        pltpu.make_async_copy(x_near.at[rows], x_rows, load_sem.at[0]).wait()

    def products_step(slot):
        @pl.loop(0, blocks)
        def _(b):
            here = lax.rem(b, 2)
            om_copy(b, here).wait()

            @pl.when(b + 1 < blocks)
            def _():
                om_copy(b + 1, 1 - here).start()

            high, low = split(x_rows[:, aligned(b * depth, depth, depth)])
            both = jnp.concatenate([high, low], axis=0)
            for n in range(TC // wide_block):
                cols = pl.ds(n * wide_block, wide_block)
                w_high, w_low = split(left[here, :, cols])
                pair = dot(both, w_high)
                value = pair[:step_rows] + pair[step_rows:] + dot(high, w_low)

                @pl.when(b == 0)
                def _():
                    partial[slot, :, cols] = value

                @pl.when(b > 0)
                def _():
                    partial[slot, :, cols] += value

    def products(s):
        load_x(s)
        if s >= 2:
            for j in range(pairs):
                pair_copy(s - 2, s % 2, j).wait_send()
        products_step(s % 2)
        for j in range(pairs):
            pair_copy(s, s % 2, j).start()
        if s + 1 < steps:
            om_copy(0, 0).start()

    def serve_x(i):
        serve(0, i)

    def serve_y(i):
        serve(1, i)

    def mix(s):
        combine(s, s % 2)

    def spread_x(_):
        xq_copy().wait_recv()
        share(2 * steps)

    def hand_far(s):
        hand_on(steps + s)

    assert steps == 2 and chunks == 8
    om_copy(0, 0).start()
    order = (
        (serve_x, 0), (serve_x, 1), (serve_x, 2), (serve_x, 3), (products, 0), (serve_x, 6), (serve_x, 7),
        (mix, 0), (finish, 0), (serve_x, 5), (hand_on, 0), (serve_x, 4), (source_step, 0), (products, 1),
        (mix, 1), (serve_y, 1), (serve_y, 0), (finish, 1), (spread_x, 0),
    )
    for action, index in order:
        action(index)
    terms = (0, 1, 4, 2, 5, 3, 6, 7)
    between = {
        1: (
            (hand_on, 1), (serve_y, 2), (serve_y, 3), (spread_far, 0), (source_step, 1), (spread_far, 1),
        ),
        3: (
            (hand_far, 0), (hand_far, 1), (hand_on, 2 * steps), (serve_y, 5), (serve_y, 6),
        ),
        5: (
            (serve_y, 4),
        ),
        6: (
            (serve_y, 7),
        ),
    }

    m_block, n_block = block_of(TR), block_of(H)
    out_blocks = TR // m_block
    halves = S // depth
    group = depth // chunk_rows

    def out_copy(i):
        rows = aligned(i * m_block, m_block, m_block)
        return pltpu.make_async_copy(acc.at[rows], acc_out.at[rows], out_sem)

    def load(src_left, src_right):
        pltpu.make_async_copy(src_left, left.at[0, :, pl.ds(0, TR)], load_sem.at[0]).start()
        pltpu.make_async_copy(src_right, right, load_sem.at[1]).start()

    def near_ref(kind, rows):
        def run(src_right):
            @pl.when(is_source)
            def _():
                load(kinds[kind][0].at[rows, tile_cols], src_right)

            @pl.when(jnp.logical_not(is_source))
            def _():
                load(kinds[kind][1].at[rows], src_right)

        return run

    def begin(place):
        u = terms[place]
        for action, index in between.get(place, ()):
            action(index)
        if u in (2, 3):
            for s in range(steps // 2):
                wait_handed(steps + (u - 2) * (steps // 2) + s)
        if u in (5, 7) and not {5, 7} & set(terms[:place]):
            wait_handed(2 * steps)
        if u in (2, 3):
            for i in range(group):
                wait_far(0, (u - 2) * group + i)
        if u in (5, 7):
            for i in range(group):
                wait_far(1, (u - 5) // 2 * group + i)
        k = u % 2 if u < 4 else (u - 4) // 2
        rows = pl.ds(k * depth, depth)
        if u < 2:
            near_ref(0, rows)(y_cols.at[rows, own_cols])
        elif u < 4:
            load(x_far.at[rows], y_cols_far.at[rows])
        elif u % 2 == 0:
            near_ref(1, rows)(samp.at[rows, own_cols])
        else:
            load(y_far.at[rows], x_cols_far.at[rows])

    assert halves == 2

    @pl.loop(0, 8)
    def _(u):
        for case in range(8):
            @pl.when(u == case)
            def _(case=case):
                begin(case)

        pltpu.make_async_copy(x_far.at[pl.ds(0, depth)], left.at[0, :, pl.ds(0, TR)], load_sem.at[0]).wait()
        pltpu.make_async_copy(y_cols_far.at[pl.ds(0, depth)], right, load_sem.at[1]).wait()
        high, low = split(right[...])
        right_high[...] = high
        right_low[...] = low

        @pl.loop(0, out_blocks)
        def _(i):
            rows = aligned(i * m_block, m_block, m_block)
            l_high, l_low = split(left[0, :, rows].T)
            for n in range(H // n_block):
                cols = pl.ds(n * n_block, n_block)
                value = dot(l_high, right_high[:, cols]) + dot(l_low, right_high[:, cols])
                value = value + dot(l_high, right_low[:, cols])

                @pl.when(u == 0)
                def _():
                    acc[rows, cols] = value

                @pl.when(u > 0)
                def _():
                    acc[rows, cols] += value

            @pl.when(u == 7)
            def _():
                out_copy(i).start()

    for i in range(chunks):
        wait_sent(0, i)
        wait_sent(1, i)

    xq_copy().wait_send()
    for which in range(2 * steps + 1):
        wait_shared(which)
    for s in range(steps):
        yq_copy(s).wait_send()
        for e in range(1, pairs):
            rs_copy(s, e).wait_send()
        if s >= steps - 2:
            for j in range(pairs):
                pair_copy(s, s % 2, j).wait_send()

    @pl.loop(0, out_blocks)
    def _(i):
        out_copy(i).wait()


def gathered(precision, samples, R, C):
    TR, TC = precision.shape
    S = samples.shape[0]
    H = TC // 2
    assert C > 2
    steps, chunks = S // step_rows, S // chunk_rows
    piece = step_rows // R
    pairs, shares = R // 2, 2 * steps + 1
    assert R % 2 == 0
    wide = max(TR, TC)
    dma = pltpu.SemaphoreType.DMA
    shapes = [(TR, H), (S, TR), (S, TR), (S, TR), (S, TR), (S, TC), (S, H), (S, H)]
    shapes.append((len(alternate) * chunk_rows, TR))
    return pl.pallas_call(
        functools.partial(gather_kernel, R, C, S, TR, TC, H),
        out_shape=[jax.ShapeDtypeStruct(shape, F32) for shape in shapes],
        in_specs=[pl.BlockSpec(memory_space=pl.ANY)] * 2,
        out_specs=[pl.BlockSpec(memory_space=pl.ANY)] * len(shapes),
        scratch_shapes=[
            pltpu.VMEM((TR, H), F32),
            pltpu.VMEM((2, depth, wide), F32),
            pltpu.VMEM((depth, H), F32),
            pltpu.VMEM((depth, H), BF16),
            pltpu.VMEM((depth, H), BF16),
            pltpu.VMEM((step_rows, TR), F32),
            pltpu.VMEM((2, step_rows, TC), F32),
            pltpu.VMEM((steps, pairs, piece, TC), F32),
            pltpu.VMEM((steps, pairs, piece, TC), F32),
            pltpu.VMEM((steps, pairs, piece, TC), F32),
            pltpu.VMEM((steps, piece, TC), F32),
            dma((2, chunks)), dma((2, chunks)), dma((2, chunks)), dma((2, chunks)), dma((2, chunks)),
            dma((len(alternate),)), dma((len(alternate),)), dma((len(alternate),)), dma((len(alternate),)),
            dma((steps, pairs)), dma((steps, pairs)), dma((steps, pairs)), dma((steps, pairs)), dma((steps,)),
            dma((shares, pairs)), dma((shares, pairs)), dma((shares, pairs)), dma((shares, pairs)),
            dma, dma, dma((steps,)), dma((steps,)),
            dma((2,)), dma((2,)), dma,
        ],
        compiler_params=pltpu.CompilerParams(
            collective_id=0, has_side_effects=True, vmem_limit_bytes=60 * 2**20
        ),
        name="gather_symmetric",
    )(precision, samples)[0]


def update_kernel(samples_total, block, ids, sym, prec, rows_o, cols_o, new_t, out, res):
    i = pl.program_id(0)
    M, H = sym.shape
    count = new_t.shape[0]

    @pl.when(i == 0)
    def _():
        res[...] = jnp.zeros_like(res)

    n_high, n_low = split(new_t[...])
    both = jnp.concatenate([n_high, n_low], axis=0)
    wide = block_of(H)
    row_id = ids[0] + i * block + lax.broadcasted_iota(jnp.int32, (M, wide), 0)
    order_rows = rows_o[...].T[:, :1]
    for n in range(H // wide):
        cols = pl.ds(n * wide, wide)
        col_id = ids[1] + n * wide + lax.broadcasted_iota(jnp.int32, (M, wide), 1)
        on_diagonal = row_id == col_id
        held = prec[:, cols]
        diag = jnp.sum(jnp.where(on_diagonal, held, 0.0), axis=0, keepdims=True)
        inverse = jnp.where(on_diagonal, 1.0 / diag, 0.0)
        gradient = sym[:, cols] / (2.0 * samples_total) - inverse
        stepped = held - step_size * gradient
        threshold = step_size * penalty * 0.5 * (order_rows + cols_o[:, cols])
        size = jnp.maximum(jnp.abs(stepped) - threshold, 0.0)
        shrunk = jnp.where(stepped < 0.0, -size, size)
        updated = jnp.where(on_diagonal, stepped, shrunk)
        out[:, cols] = updated
        u_high, u_low = split(updated)
        pair = dot(both, u_high)
        value = pair[:count] + pair[count:] + dot(n_high, u_low)
        res[pl.ds(0, count), cols] += value
        res[pl.ds(count, 8), cols] += jnp.broadcast_to(diag, (8, wide))


def updated_and_partial(symmetric, precision, new_rows, orders_rows, orders_cols, ids, half_index, samples_total):
    TR, H = symmetric.shape
    count = new_rows.shape[0]
    block = 256

    return pl.pallas_call(
        functools.partial(update_kernel, samples_total, block),
        out_shape=[jax.ShapeDtypeStruct((TR, H), F32), jax.ShapeDtypeStruct((count + 8, H), F32)],
        grid_spec=pltpu.PrefetchScalarGridSpec(
            num_scalar_prefetch=1,
            grid=(TR // block,),
            in_specs=[
                pl.BlockSpec((block, H), lambda i, ids: (i, 0)),
                pl.BlockSpec((block, H), lambda i, ids: (i, ids[2])),
                pl.BlockSpec((8, block), lambda i, ids: (0, i)),
                pl.BlockSpec((1, H), lambda i, ids: (0, 0)),
                pl.BlockSpec((count, block), lambda i, ids: (0, i)),
            ],
            out_specs=[
                pl.BlockSpec((block, H), lambda i, ids: (i, 0)),
                pl.BlockSpec((count + 8, H), lambda i, ids: (0, 0)),
            ],
        ),
        compiler_params=pltpu.CompilerParams(vmem_limit_bytes=56 * 2**20),
        name="update_rows",
    )(ids, symmetric, precision, orders_rows, orders_cols, new_rows)


def residual_kernel(R, part, out, held, got, diags, send, recv, diag_send, diag_recv):
    r, z, p = lax.axis_index("row"), lax.axis_index("col"), lax.axis_index("rep")
    rows = out.shape[0]
    rounds = R.bit_length() - 1

    def flip(bit):
        low = lax.rem(r // bit, 2)
        return r + bit - 2 * bit * low

    barrier = pltpu.get_barrier_semaphore()
    for d in range(1, R):
        where = (lax.rem(r + d, R), z, p)
        pl.semaphore_signal(barrier, inc=1, device_id=where, device_id_type=MESH)
    pl.semaphore_wait(barrier, R - 1)

    def diag_copy(d):
        where = (lax.rem(r + d, R), z, p)
        return pltpu.make_async_remote_copy(
            src_ref=part.at[pl.ds(rows * R, 8)], dst_ref=diags.at[d - 1], send_sem=diag_send.at[d],
            recv_sem=diag_recv.at[d], device_id=where, device_id_type=MESH)

    def exchange(stage, j):
        bit = 1 << stage
        peer = flip(bit)
        block = lax.rem(peer, 2 * bit) + 2 * bit * j
        src = part if stage == 0 else held
        return pltpu.make_async_remote_copy(
            src_ref=src.at[aligned(block * rows, rows, 8)], dst_ref=got.at[stage, j],
            send_sem=send.at[stage, j], recv_sem=recv.at[stage, j],
            device_id=(peer, z, p), device_id_type=MESH)

    count = [R >> (stage + 1) for stage in range(rounds)]
    def ranked(stage):
        if stage + 1 == rounds:
            return [0], []
        own = lax.rem(r // (2 << stage), 2)
        first = [2 * j + 1 - own for j in range(count[stage + 1])]
        return first, [2 * j + own for j in range(count[stage + 1])]

    for j in sum(ranked(0), []):
        exchange(0, j).start()
    for d in range(1, R):
        diag_copy(d).start()
    for stage in range(rounds):
        bit = 1 << stage

        def receive(j, stage=stage, bit=bit):
            mine = lax.rem(r, 2 * bit) + 2 * bit * j
            block = aligned(mine * rows, rows, 8)
            exchange(stage, j).wait_recv()
            src = part if stage == 0 else held
            held[block] = src[block] + got[stage, j]

        first, second = ranked(stage)
        for j, index in enumerate(first):
            receive(index)
            if stage + 1 < rounds:
                exchange(stage + 1, j).start()
        for index in second:
            receive(index)
    diag = part[pl.ds(rows * R, 1)]
    for d in range(1, R):
        diag_copy(d).wait_recv()
        diag = diag + diags[d - 1, pl.ds(0, 1)]
    out[...] = held[aligned(r * rows, rows, 8)] / diag
    for stage in range(rounds):
        for j in range(count[stage]):
            exchange(stage, j).wait_send()
    for d in range(1, R):
        diag_copy(d).wait_send()


def residual_sum(part, R):
    total, H = part.shape
    rows = (total - 8) // R
    assert R & (R - 1) == 0
    rounds = R.bit_length() - 1
    dma = pltpu.SemaphoreType.DMA
    return pl.pallas_call(
        functools.partial(residual_kernel, R),
        out_shape=jax.ShapeDtypeStruct((rows, H), F32),
        in_specs=[pl.BlockSpec(memory_space=pltpu.VMEM)],
        out_specs=pl.BlockSpec(memory_space=pltpu.VMEM),
        scratch_shapes=[
            pltpu.VMEM((R * rows, H), F32),
            pltpu.VMEM((rounds, R // 2, rows, H), F32),
            pltpu.VMEM((R - 1, 8, H), F32),
            dma((rounds, R // 2)), dma((rounds, R // 2)), dma((R,)), dma((R,)),
        ],
        compiler_params=pltpu.CompilerParams(
            collective_id=1, has_side_effects=True, vmem_limit_bytes=40 * 2**20
        ),
        name="residual_sum",
    )(part)


def per_device(precision, samples, new_rows, ngram_order):
    R, C, reps = lax.axis_size("row"), lax.axis_size("col"), lax.axis_size("rep")
    r, c, p = lax.axis_index("row"), lax.axis_index("col"), lax.axis_index("rep")
    TR, TC = precision.shape
    H = TC // reps
    assert reps == 2 and TC % TR == 0 and R * TR == C * TC
    symmetric = gathered(precision, samples, R, C)
    orders = ngram_order.astype(F32)
    row_start, col_start = r * TR, c * TC + p * H
    order_rows = jnp.broadcast_to(lax.dynamic_slice_in_dim(orders, row_start, TR, 0)[None, :], (8, TR))
    order_cols = lax.dynamic_slice_in_dim(orders, col_start, H, 0)[None, :]
    ids = jnp.stack([row_start, col_start, p]).astype(jnp.int32)
    updated, part = updated_and_partial(
        symmetric, precision, new_rows, order_rows, order_cols, ids, p, samples.shape[0] * reps
    )
    return updated, residual_sum(part, R)


def solution(mesh):
    placed = (P("row", "col"), P("rep", "col"), P(None, "row"), P())
    return jax.shard_map(
        per_device,
        mesh=mesh,
        in_specs=placed,
        out_specs=(P("row", ("col", "rep")), P("row", ("col", "rep"))),
        check_vma=False,
    )
```
